128 devices in a mesh: batch: 4 (over x), span: 32 (over z, y, core).
Axes of the slice: x: 4, y: 4, z: 4, core: 2. Of those that a mesh axis runs over, the one named last changes fastest.
Arguments:
- heads_in: bfloat16 [131072, 1536], P(('batch', 'span')), parts along dimension 0, may hold values from -6 to 6
- writer: bfloat16 [131072, 64], P(('batch', 'span')), parts along dimension 0, may hold values from -6 to 6
- reader: bfloat16 [131072, 64], P(('batch', 'span')), parts along dimension 0, may hold values from -6 to 6
- log_decay: float32 [131072, 48], P(('batch', 'span')), parts along dimension 0, may hold values from -1 to 0
- norm_gain: float32 [1536], replicated, may hold values from 0.1 to 1.9
- merge_weight: bfloat16 [6144, 1536], replicated, may hold values from -0.078125 to 0.078125
- frame_owner: int32 [2048], P(('batch', 'span')), parts along dimension 0, may hold values from 0 to 31, as said below
Outputs:
- placed: bfloat16 [65536, 1536], P(('batch', 'span')), parts along dimension 0
The draws below stay inside these ranges and needn't reach their ends.
There are 4 independent parts, one for each index of `batch`. The reference program is written for one: setup_inputs(seed, part) draws one part's arguments, and reference() takes and returns one part's arrays. A program takes and returns all parts, laid end to end along the dimension named above; an argument that names none is the same for every part. Nothing has to cross between parts.
Inputs may be any that keep to these rules, and one draw needn't show every extreme that they name: `frame_owner`: the 16 frames of one index of span go to 16 different owners. One owner receives at most 32 frames of a video, and some owner receives exactly 32.
All inputs are finite; a program needn't handle non-finite values.
Results may differ from the reference program's by a relative error of at most 0.0061.
Values may be sent and summed in bfloat16 or wider, within the bound.
A program may use at most 128 MiB of HBM per device.

```python
import math
import jax
import jax.numpy as jnp
from jax import lax

HEADS = 48
STATE = 64
LLM_WIDTH = 1536
FRAME_SIDE = 8
F_DEV = 16
WIDTH = 1536
MROWS = 16
TOK_DEV = 1024
BLOCK = 512
VIDEO_TOKENS = 32768
FRAMES = 512
CAP = 32
N_SPAN = 32


def draw_frame_owner(key, part):
    owners = FRAMES // F_DEV
    spread = min(F_DEV, owners - F_DEV)
    shifts = jax.random.randint(jax.random.fold_in(key, 11), (owners // 2,), 0, spread + 1)
    shifts = shifts.at[0].set(spread)
    counts = jnp.stack([F_DEV + shifts, F_DEV - shifts], axis=1).reshape(owners)
    ordering = jax.random.permutation(jax.random.fold_in(key, 12), owners).astype(jnp.int32)
    limits = jnp.cumsum(counts)
    ticket = jnp.arange(FRAMES, dtype=jnp.int32)
    position = jnp.sum((limits[None, :] <= ticket[:, None]).astype(jnp.int32), axis=1)
    holder = ordering[position]
    return holder.reshape(F_DEV, owners).T.reshape(FRAMES).astype(jnp.int32)


def draw_log_decay(key, part):
    head_pairs = HEADS // 2
    pair_rank = jax.random.permutation(jax.random.fold_in(key, 21), head_pairs)
    fast_pairs = head_pairs // 2
    quick_head = jnp.repeat(pair_rank < fast_pairs, 2)
    fast_rate = jax.random.uniform(jax.random.fold_in(key, 22), (HEADS,), minval=0.02, maxval=0.035)
    slow_total = jnp.exp(jax.random.uniform(jax.random.fold_in(key, 23), (HEADS,), minval=math.log(0.05), maxval=math.log(0.8)))
    baseline_rate = jnp.where(quick_head, fast_rate, slow_total / VIDEO_TOKENS)
    jaggedness = jax.random.uniform(jax.random.fold_in(key, 24), (VIDEO_TOKENS, HEADS), minval=0.5, maxval=1.5)
    devices = VIDEO_TOKENS // TOK_DEV
    multiplier = jnp.exp(jax.random.uniform(jax.random.fold_in(key, 25), (devices, HEADS), minval=math.log(0.5), maxval=math.log(2.0)))
    multiplier = jnp.repeat(multiplier, TOK_DEV, axis=0)
    spike_position = jax.random.randint(jax.random.fold_in(key, 26), (3,), 0, VIDEO_TOKENS)
    affected_rows = jnp.any(jnp.arange(VIDEO_TOKENS)[:, None] == spike_position[None, :], axis=1)
    discard_size = jax.random.uniform(jax.random.fold_in(key, 27), (VIDEO_TOKENS, HEADS), minval=0.22, maxval=0.69)
    spike_penalty = jnp.where(affected_rows[:, None] & jnp.logical_not(quick_head)[None, :], discard_size, 0.0)
    return (-(baseline_rate[None, :] * jaggedness * multiplier + spike_penalty)).astype(jnp.float32)


def block_scale(rng, dims, cuts, low, high):
    def one(axis_at, shards_of):
        draws = jax.random.uniform(jax.random.fold_in(jax.random.fold_in(rng, 6), axis_at), (shards_of,), jnp.float32, low / len(cuts), high / len(cuts))
        return jnp.repeat(jnp.exp(draws), dims[axis_at] // shards_of).reshape((-1,) + (1,) * (len(dims) - axis_at - 1))

    factor_of = one(*cuts[0])
    for cut in cuts[1:]:
        factor_of = factor_of * one(*cut)
    return factor_of


def normal_values(key, extent, scale, reach, shards=(), kind=jnp.bfloat16):
    result = jax.random.normal(key, extent, jnp.float32) * scale
    if len(shards) > 0:
        result = block_scale(key, extent, shards, -0.22, 0.18) * result
    return jnp.clip(result, min=-reach, max=reach).astype(kind)


def setup_inputs(seed: int = 0, part: int = 0) -> dict:
    keys = jax.random.split(jax.random.key(seed), 8)
    part_keys = jax.random.split(jax.random.fold_in(keys[7], part), 8)
    heads_in = normal_values(part_keys[0], (VIDEO_TOKENS, WIDTH), 1.0, 6.0, ((0, 32),))
    writer = normal_values(part_keys[1], (VIDEO_TOKENS, STATE), 1.0, 6.0, ((0, 32),))
    reader = normal_values(part_keys[2], (VIDEO_TOKENS, STATE), 1.0, 6.0, ((0, 32),))
    log_decay = draw_log_decay(jax.random.fold_in(jax.random.fold_in(keys[7], part), 71), part)
    norm_gain = jnp.clip(1.0 + 0.18 * jax.random.normal(keys[4], (WIDTH,), jnp.float32), 0.1, 1.9)
    merge_weight = normal_values(keys[5], (4 * WIDTH, LLM_WIDTH), (4 * WIDTH) ** -0.5, 0.078125)
    frame_owner = draw_frame_owner(jax.random.fold_in(jax.random.fold_in(keys[7], part), 71), part)
    return {"heads_in": heads_in, "writer": writer, "reader": reader, "log_decay": log_decay, "norm_gain": norm_gain, "merge_weight": merge_weight, "frame_owner": frame_owner}


epsilon = 1e-05

def block_terms(x_blk, write_blk, read_blk, decay_blk, heads, head_dim):
    length, width = x_blk.shape
    running = jnp.cumsum(decay_blk, axis=0)
    running_heads = running.T
    scores = jnp.dot(read_blk, write_blk.T, preferred_element_type=jnp.float32)
    row_index = lax.broadcasted_iota(jnp.int32, (length, length), 0)
    col_index = lax.broadcasted_iota(jnp.int32, (length, length), 1)
    causal = row_index >= col_index
    spacing = running_heads[:, :, None] - running_heads[:, None, :]
    spacing = jnp.where(causal[None], spacing, -jnp.inf)
    weights = (scores[None] * jnp.exp(spacing)).astype(jnp.bfloat16)
    values = x_blk.reshape(length, heads, head_dim).astype(jnp.float32)
    within = jnp.einsum('hts,shp->thp', weights.astype(jnp.float32), values).reshape(length, width)
    to_end = jnp.exp(running[-1:, :] - running)
    scaled = (values * to_end[:, :, None]).astype(jnp.bfloat16).reshape(length, width)
    block_state = jnp.dot(write_blk.T, scaled, preferred_element_type=jnp.float32)
    block_decay = jnp.exp(running[-1])
    return (within, block_state, block_decay, jnp.exp(running))

def carried(read_blk, carry_state, from_start, head_dim):
    rounded = carry_state.astype(jnp.bfloat16)
    projected = jnp.dot(read_blk, rounded, preferred_element_type=jnp.float32)
    return projected * jnp.repeat(from_start, head_dim, axis=1)

def group_norm(mixed, norm_gain, head_dim):
    length, width = mixed.shape
    grouped = mixed.reshape(length, width // (2 * head_dim), 2 * head_dim)
    square_mean = lax.optimization_barrier(jnp.mean(grouped * grouped, axis=-1, keepdims=True))
    scaled = (grouped * lax.rsqrt(square_mean + epsilon)).reshape(length, width)
    return (scaled * norm_gain[None, :]).astype(jnp.bfloat16)

def shuffle(normed, frame_side):
    width = normed.shape[1]
    half = frame_side // 2
    cells = normed.reshape(-1, half, 2, half, 2, width)
    cells = jnp.transpose(cells, (0, 1, 3, 2, 4, 5))
    return cells.reshape(-1, 4 * width)

def reference(heads_in, writer, reader, log_decay, norm_gain, merge_weight, frame_owner):
    heads = log_decay.shape[1]
    width = heads_in.shape[1]
    head_dim = width // heads
    blocks = VIDEO_TOKENS // BLOCK
    input_blocks = heads_in.reshape(blocks, BLOCK, width)
    write_blocks = writer.reshape(blocks, BLOCK, STATE)
    read_blocks = reader.reshape(blocks, BLOCK, STATE)
    decay_blocks = log_decay.reshape(blocks, BLOCK, heads)

    def advance_block(carry_state, block_items):
        x_blk, write_blk, read_blk, decay_blk = block_items
        within, block_state, block_decay, from_start = block_terms(x_blk, write_blk, read_blk, decay_blk, heads, head_dim)
        output = within + carried(read_blk, carry_state, from_start, head_dim)
        carry_state = carry_state * jnp.repeat(block_decay, head_dim)[None, :] + block_state
        return (carry_state, output)
    start_state = jnp.zeros((STATE, width), jnp.float32)
    _, mixed = lax.scan(advance_block, start_state, (input_blocks, write_blocks, read_blocks, decay_blocks))
    mixed = mixed.reshape(VIDEO_TOKENS, width)
    normed = group_norm(mixed, norm_gain, head_dim)
    shuffled = shuffle(normed, FRAME_SIDE)
    merged = jnp.dot(shuffled, merge_weight, preferred_element_type=jnp.float32).astype(jnp.bfloat16)
    merged = merged.reshape(FRAMES, MROWS, LLM_WIDTH)
    same_owner = frame_owner[:, None] == frame_owner[None, :]
    row_index = lax.broadcasted_iota(jnp.int32, (FRAMES, FRAMES), 0)
    col_index = lax.broadcasted_iota(jnp.int32, (FRAMES, FRAMES), 1)
    earlier = col_index < row_index
    frame_rank = lax.optimization_barrier(jnp.sum((same_owner & earlier).astype(jnp.int32), axis=1))
    target = (frame_owner * CAP + frame_rank).astype(jnp.int32)
    placed = jnp.zeros((N_SPAN * CAP, MROWS, LLM_WIDTH), jnp.bfloat16).at[target].set(merged)
    return placed.reshape(N_SPAN * CAP * MROWS, LLM_WIDTH)
```

```python
import functools

import jax
import jax.numpy as jnp
from jax import lax
from jax.experimental import pallas as pl
from jax.experimental.pallas import tpu as pltpu
from jax.sharding import PartitionSpec as P

MESH = pl.DeviceIdType.MESH
F32 = jnp.float32
BF16 = jnp.bfloat16
EPSILON = 1e-05
FRAME_SIDE = 8
CHUNK = 128
LANES = 256
GROUP = 64


def dot(a, b):
    return lax.dot_general(a, b, (((1,), (0,)), ((), ())), preferred_element_type=F32)


def iota(shape, axis):
    return lax.broadcasted_iota(jnp.int32, shape, axis)


def ones_where(condition):
    return jnp.where(condition, 1.0, 0.0).astype(BF16)


def token_of_row(row):
    q, rest = row >> 5, row & 31
    frame, i2, j2 = rest >> 4, (rest >> 2) & 3, rest & 3
    return frame * 64 + (2 * i2 + (q >> 1)) * 8 + 2 * j2 + (q & 1)


def two_parts(values):
    high = values.astype(BF16)
    low = (values - high.astype(F32)).astype(BF16)
    return jnp.where(iota(values.shape, 1) < 64, high.astype(F32), low.astype(F32)).astype(BF16)


def kernel(
    n, x_h, w_h, r_h, d_h, g_h, o_h, wm_h, out_h,
    x_v, w_v, r_v, d_v, g_v, o_v, wm_v,
    cum_l, expand, block_diag, perm, xs_v, out_arg, dev_arg, state, rp_v, ml_v, od_v, a_v,
    meta_s, meta_r, send1, recv1, decays, send2, recv2, enter, sel_s, sel_r, send3, recv3, out_v,
    x_sem, in_sem, wm_sem, out_sem, meta_sem, one_sem, two_sem, del_s_sem, del_r_sem,
):
    me = lax.axis_index("span")
    chunks, _, width = x_v.shape
    heads = d_h.shape[1]
    tiles = width // LANES
    frames = o_h.shape[1]
    rows = 16

    small = [
        pltpu.make_async_copy(s, d, in_sem.at[k])
        for k, (s, d) in enumerate(((d_h, d_v), (w_h, w_v), (r_h, r_v), (g_h, g_v), (o_h, o_v)))
    ]
    loads = [pltpu.make_async_copy(x_h.at[c], x_v.at[c], x_sem.at[c]) for c in range(chunks)]
    weights = [
        pltpu.make_async_copy(wm_h.at[:, pl.ds(t * LANES, LANES)], wm_v.at[t], wm_sem.at[t])
        for t in range(tiles)
    ]
    for copy in small + loads + weights:
        copy.start()

    barrier = pltpu.get_barrier_semaphore()

    def greet(k, _):
        pl.semaphore_signal(
            barrier, inc=1, device_id={"span": lax.rem(me + k, n)}, device_id_type=MESH
        )
        return 0

    lax.fori_loop(1, n, greet, 0)

    row_l, col_l = iota((CHUNK, CHUNK), 0), iota((CHUNK, CHUNK), 1)
    token = token_of_row(row_l)
    lower = ones_where(col_l <= row_l)
    lower_p = ones_where(col_l <= token)
    perm[...] = ones_where(col_l == token)
    for k in range(3):
        cum_l[0:CHUNK, k * CHUNK : (k + 1) * CHUNK] = lower
        cum_l[CHUNK : 2 * CHUNK, k * CHUNK : (k + 1) * CHUNK] = lower_p
    head_dim_shift = (width // heads).bit_length() - 1
    expand[...] = ones_where(
        (iota((128, width), 0) & 63) == (iota((128, width), 1) >> head_dim_shift)
    )
    block_diag[...] = ones_where(
        (iota((LANES, LANES), 0) >> 6) == (iota((LANES, LANES), 1) >> 6)
    )
    state[...] = jnp.zeros_like(state)
    meta_s[...] = jnp.full(meta_s.shape, -1.0, F32)
    for copy in small:
        copy.wait()

    owners = o_v[...].astype(F32)
    meta_s[1:2, 0:frames] = owners
    owner_rows = jnp.broadcast_to(owners, (8, frames)).astype(BF16)
    spread = ones_where(
        iota((frames, frames * rows), 0) == (iota((frames, frames * rows), 1) >> 4)
    )
    owner_row = dot(owner_rows, spread)[0:1]
    shape = (n * rows, frames * rows)
    sel_s[...] = ones_where(
        ((iota(shape, 0) >> 4).astype(F32) == owner_row)
        & ((iota(shape, 0) & 15) == (iota(shape, 1) & 15))
    )

    def summarize(c, before):
        start = pl.multiple_of(c * CHUNK, CHUNK)
        decay = d_v[pl.ds(start, CHUNK), :]
        gap = jnp.zeros((CHUNK, 64 - heads), F32)
        decay = jnp.concatenate([decay, gap, decay, gap], axis=1)
        high = decay.astype(BF16)
        left = decay - high.astype(F32)
        middle = left.astype(BF16)
        low = (left - middle.astype(F32)).astype(BF16)
        both = dot(cum_l[...], jnp.concatenate([high, middle, low], axis=0))
        running, running_p = both[0:CHUNK], both[CHUNK : 2 * CHUNK]
        ref = running[CHUNK // 2 - 1 : CHUNK // 2]
        total = running[CHUNK - 1 : CHUNK]
        out_arg[c] = running_p - ref
        dev_arg[c] = running_p + before
        row = iota((16, 128), 0)
        extra = jnp.where(row == 0, ref, jnp.where(row == 1, total, total - ref))
        factors = two_parts(jnp.exp(jnp.concatenate([ref - running, extra], axis=0)))
        writes = w_v[pl.ds(start, CHUNK), :]
        pltpu.make_async_copy(x_h.at[c], x_v.at[c], x_sem.at[c]).wait()
        for t in range(tiles):
            cols = slice(t * LANES, (t + 1) * LANES)
            full = dot(factors, expand[:, cols])
            scaled = (x_v[c, :, cols].astype(F32) * full[0:CHUNK]).astype(BF16)
            own = lax.dot_general(
                writes, scaled, (((0,), (0,)), ((), ())), preferred_element_type=F32
            )
            earlier = state[:, cols]
            xs_v[c, t, 0:CHUNK] = scaled
            xs_v[c, t, CHUNK : CHUNK + 64] = (earlier * full[CHUNK : CHUNK + 1]).astype(BF16)
            state[:, cols] = (
                earlier * full[CHUNK + 1 : CHUNK + 2] + own * full[CHUNK + 2 : CHUNK + 3]
            )
        return before + total

    total = lax.fori_loop(0, chunks, summarize, jnp.zeros((1, 128), F32))
    meta_s[0:1, :] = total
    for a in range(8):
        for b in range(4):
            send1[a * 4 + b] = state[8 * a : 8 * a + 8, 384 * b : 384 * b + 384].astype(BF16)

    pl.semaphore_wait(barrier, n - 1)

    def remote(source, target, sems, d):
        return pltpu.make_async_remote_copy(
            src_ref=source,
            dst_ref=target,
            send_sem=sems.at[0],
            recv_sem=sems.at[1],
            device_id={"span": d},
            device_id_type=MESH,
        )

    def all_of(ref, sem):
        part = ref.at[pl.ds(0, n - 1)]
        pltpu.make_async_copy(part, part, sem).wait()

    def send_meta(k, _):
        remote(meta_s, meta_r.at[me], meta_sem, lax.rem(me + k, n)).start()
        return 0

    lax.fori_loop(1, n, send_meta, 0)

    def send_one(k, _):
        d = lax.rem(me + k, n)
        remote(send1.at[d], recv1.at[me], one_sem, d).start()
        return 0

    lax.fori_loop(1, n, send_one, 0)
    meta_r[me] = meta_s[...]
    recv1[me] = send1[me]

    causal = iota((CHUNK, CHUNK), 1) <= token_of_row(iota((CHUNK, CHUNK), 0))

    def local(c, _):
        start = pl.multiple_of(c * CHUNK, CHUNK)
        reads = dot(perm[...], r_v[pl.ds(start, CHUNK), :]).astype(BF16)
        rp_v[pl.ds(start, CHUNK), :] = reads
        scores = lax.dot_general(
            reads, w_v[pl.ds(start, CHUNK), :], (((1,), (1,)), ((), ())),
            preferred_element_type=F32,
        )
        masked = jnp.where(causal, scores, 0.0).astype(BF16)
        left = jnp.concatenate([masked, reads], axis=1)
        factors = two_parts(jnp.exp(jnp.concatenate([out_arg[c], dev_arg[c]], axis=0)))
        for t in range(tiles):
            full = dot(factors, expand[:, t * LANES : (t + 1) * LANES])
            mixed = dot(left, xs_v[c, t])
            ml_v[t, pl.ds(start, CHUNK), :] = mixed * full[0:CHUNK]
            od_v[t, pl.ds(start, CHUNK), :] = full[CHUNK : 2 * CHUNK]
        return 0

    lax.fori_loop(0, chunks, local, 0)

    all_of(meta_r, meta_sem.at[1])
    totals = meta_r[:, 0, :]
    factors = two_parts(jnp.exp(totals))
    for b in range(4):
        decays[b] = dot(factors, expand[:, 384 * b : 384 * b + 384])
    owned = jnp.max(jnp.where(meta_r[:, 1, :] == me.astype(F32), 1.0, 0.0), axis=1, keepdims=True)
    owned = jnp.broadcast_to(owned, (n, 128))
    rank = dot(ones_where(iota((n, n), 1) < iota((n, n), 0)), owned.astype(BF16))
    place = jnp.where(owned > 0.0, rank + 1.0, 0.0)[:, 0:1]
    shape = (n, n * rows)
    place_row = jnp.sum(
        jnp.where((iota(shape, 1) >> 4) == iota(shape, 0), place, 0.0), axis=0, keepdims=True
    )
    shape = (n * rows, n * rows)
    sel_r[...] = ones_where(
        (((iota(shape, 0) >> 4) + 1).astype(F32) == place_row)
        & ((iota(shape, 0) & 15) == (iota(shape, 1) & 15))
    )

    all_of(recv1, one_sem.at[1])
    quarter = lax.rem(me, 4)
    carry = jnp.zeros(recv1.shape[1:], F32)
    for i in range(n):
        send2[i] = carry.astype(BF16)
        if i < n - 1:
            carry = carry * decays[quarter, i : i + 1, :] + recv1[i].astype(F32)

    def send_two(k, _):
        d = lax.rem(me + k, n)
        remote(send2.at[d], recv2.at[me], two_sem, d).start()
        return 0

    lax.fori_loop(1, n, send_two, 0)
    recv2[me] = send2[me]
    all_of(recv2, two_sem.at[1])
    for a in range(8):
        for b in range(4):
            enter[8 * a : 8 * a + 8, 384 * b : 384 * b + 384] = recv2[a * 4 + b].astype(F32)

    def norm(t, _):
        first = pl.multiple_of(t * LANES, LANES)
        entering = enter[:, pl.ds(first, LANES)].astype(BF16)
        gain = g_v[:, pl.ds(first, LANES)]
        for b in range(chunks // 2):
            part = slice(2 * b * CHUNK, 2 * (b + 1) * CHUNK)
            mixed = ml_v[t, part] + od_v[t, part] * dot(rp_v[part], entering)
            squares = dot((mixed * mixed).astype(BF16), block_diag[...])
            normed = mixed * lax.rsqrt(squares * (1.0 / GROUP) + EPSILON) * gain
            normed = normed.astype(BF16)
            for c in range(2):
                for q in range(4):
                    a_v[
                        (2 * b + c) * 32 : (2 * b + c + 1) * 32,
                        pl.ds(pl.multiple_of(q * width + t * LANES, LANES), LANES),
                    ] = normed[c * CHUNK + q * 32 : c * CHUNK + (q + 1) * 32]
        return 0

    lax.fori_loop(0, tiles, norm, 0)

    def deliver(t, _):
        pltpu.make_async_copy(
            wm_h.at[:, pl.ds(pl.multiple_of(t * LANES, LANES), LANES)], wm_v.at[t], wm_sem.at[t]
        ).wait()
        merged = dot(a_v[...], wm_v[t]).astype(BF16)
        send3[t] = dot(sel_s[...], merged).astype(BF16).reshape(n, rows, LANES)

        def send(k, _):
            d = lax.rem(me + k, n)
            pltpu.make_async_remote_copy(
                src_ref=send3.at[t, d],
                dst_ref=recv3.at[t, me],
                send_sem=del_s_sem,
                recv_sem=del_r_sem.at[t],
                device_id={"span": d},
                device_id_type=MESH,
            ).start()
            return 0

        lax.fori_loop(1, n, send, 0)
        recv3[t, me] = send3[t, me]
        return 0

    lax.fori_loop(0, tiles, deliver, 0)

    def put(t):
        return pltpu.make_async_copy(
            out_v.at[t], out_h.at[:, pl.ds(pl.multiple_of(t * LANES, LANES), LANES)], out_sem
        )

    def arrive(t, _):
        part = recv3.at[t, pl.ds(0, n - 1)]
        pltpu.make_async_copy(part, part, del_r_sem.at[t]).wait()
        out_v[t] = dot(sel_r[...], recv3[t].reshape(n * rows, LANES)).astype(BF16)
        put(t).start()
        return 0

    lax.fori_loop(0, tiles, arrive, 0)
    pltpu.make_async_copy(out_v, out_v, out_sem).wait()
    one_meta = meta_r.at[pl.ds(0, n - 1)]
    pltpu.make_async_copy(one_meta, one_meta, meta_sem.at[0]).wait()
    all_of(send1, one_sem.at[0])
    all_of(send2, two_sem.at[0])

    def sent(t, _):
        part = send3.at[t, pl.ds(0, n - 1)]
        pltpu.make_async_copy(part, part, del_s_sem).wait()
        return 0

    lax.fori_loop(0, tiles, sent, 0)


def shards(heads_in, writer, reader, log_decay, norm_gain, merge_weight, frame_owner):
    tokens, width = heads_in.shape
    n = lax.axis_size("span")
    chunks = tokens // CHUNK
    tiles = width // LANES
    frames = frame_owner.shape[0]
    state_size = writer.shape[1]
    deep, out_width = merge_weight.shape
    assert (n, state_size, width, out_width, frames) == (32, 64, 1536, 1536, 16)
    vmem, dma = pltpu.VMEM, pltpu.SemaphoreType.DMA
    anywhere = pl.BlockSpec(memory_space=pl.ANY)
    return pl.pallas_call(
        functools.partial(kernel, n),
        out_shape=jax.ShapeDtypeStruct((n * 16, out_width), BF16),
        in_specs=[anywhere] * 7,
        out_specs=anywhere,
        scratch_shapes=[
            vmem((chunks, CHUNK, width), BF16),
            vmem(writer.shape, BF16),
            vmem(reader.shape, BF16),
            vmem(log_decay.shape, F32),
            vmem((1, width), F32),
            vmem((1, frames), jnp.int32),
            vmem((tiles, deep, LANES), BF16),
            vmem((2 * CHUNK, 3 * CHUNK), BF16),
            vmem((128, width), BF16),
            vmem((LANES, LANES), BF16),
            vmem((CHUNK, CHUNK), BF16),
            vmem((chunks, tiles, CHUNK + state_size, LANES), BF16),
            vmem((chunks, CHUNK, 128), F32),
            vmem((chunks, CHUNK, 128), F32),
            vmem((state_size, width), F32),
            vmem((tokens, state_size), BF16),
            vmem((tiles, tokens, LANES), F32),
            vmem((tiles, tokens, LANES), F32),
            vmem((tokens // 4, deep), BF16),
            vmem((8, 128), F32),
            vmem((n, 8, 128), F32),
            vmem((n, 8, 384), BF16),
            vmem((n, 8, 384), BF16),
            vmem((4, n, 384), F32),
            vmem((n, 8, 384), BF16),
            vmem((n, 8, 384), BF16),
            vmem((state_size, width), F32),
            vmem((n * 16, frames * 16), BF16),
            vmem((n * 16, n * 16), BF16),
            vmem((tiles, n, 16, LANES), BF16),
            vmem((tiles, n, 16, LANES), BF16),
            vmem((tiles, n * 16, LANES), BF16),
            dma((chunks,)),
            dma((5,)),
            dma((tiles,)),
            dma,
            dma((2,)),
            dma((2,)),
            dma((2,)),
            dma,
            dma((tiles,)),
        ],
        compiler_params=pltpu.CompilerParams(
            collective_id=0, has_side_effects=True, vmem_limit_bytes=62 * 1024 * 1024
        ),
    )(
        heads_in.reshape(chunks, CHUNK, width),
        writer,
        reader,
        log_decay,
        norm_gain.reshape(1, width),
        frame_owner.reshape(1, frames),
        merge_weight,
    )


def solution(mesh):
    return jax.shard_map(
        shards,
        mesh=mesh,
        in_specs=(
            P(("batch", "span"), None),
            P(("batch", "span"), None),
            P(("batch", "span"), None),
            P(("batch", "span"), None),
            P(),
            P(),
            P(("batch", "span")),
        ),
        out_specs=P(("batch", "span"), None),
        check_vma=False,
    )
```

```python
import functools

import jax
import jax.numpy as jnp
from jax import lax
from jax.experimental import pallas as pl
from jax.experimental.pallas import tpu as pltpu
from jax.sharding import PartitionSpec as P

MESH = pl.DeviceIdType.MESH
F32 = jnp.float32
BF16 = jnp.bfloat16
EPSILON = 1e-05
FRAME_SIDE = 8
CHUNK = 128
LANES = 256
GROUP = 64


def dot(a, b):
    return lax.dot_general(a, b, (((1,), (0,)), ((), ())), preferred_element_type=F32)


def dot_t(a, b):
    return lax.dot_general(a, b, (((1,), (1,)), ((), ())), preferred_element_type=F32)


def iota(shape, axis):
    return lax.broadcasted_iota(jnp.int32, shape, axis)


def ones_where(condition):
    return jnp.where(condition, 1.0, 0.0).astype(BF16)


def token_of_row(row):
    q, rest = row >> 5, row & 31
    frame, i2, j2 = rest >> 4, (rest >> 2) & 3, rest & 3
    return frame * 64 + (2 * i2 + (q >> 1)) * 8 + 2 * j2 + (q & 1)


def two_parts(values):
    high = values.astype(BF16)
    low = (values - high.astype(F32)).astype(BF16)
    return jnp.where(iota(values.shape, 1) < 64, high.astype(F32), low.astype(F32)).astype(BF16)


def kernel(
    n, x_h, w_h, r_h, d_h, g_h, o_h, wm_h, out_h,
    x_v, w_v, r_v, d_v, g_v, o_v, wm_v,
    cum_l, expand, block_diag, perm, xs_v, out_arg, dev_arg, state, rp_v, ml_v, od_v, a_v,
    meta_s, meta_r, send1, recv1, decays, send2, recv2, enter, sel_s, sel_r, send3, recv3,
    x_sem, in_sem, wm_sem, meta_sem, one_sem, two_sem, del_s_sem, del_r_sem,
):
    me = lax.axis_index("span")
    chunks, _, width = x_v.shape
    heads = d_h.shape[0]
    tiles = width // LANES
    frames = o_h.shape[1]
    rows = 16

    small = [
        pltpu.make_async_copy(s, d, in_sem.at[k])
        for k, (s, d) in enumerate(((d_h, d_v), (w_h, w_v), (r_h, r_v), (g_h, g_v), (o_h, o_v)))
    ]
    loads = [pltpu.make_async_copy(x_h.at[c], x_v.at[c], x_sem.at[c]) for c in range(chunks)]
    weights = [
        pltpu.make_async_copy(wm_h.at[:, pl.ds(t * LANES, LANES)], wm_v.at[t], wm_sem.at[t])
        for t in range(tiles)
    ]
    for copy in small + loads + weights:
        copy.start()

    barrier = pltpu.get_barrier_semaphore()

    def greet(k, _):
        pl.semaphore_signal(
            barrier, inc=1, device_id={"span": lax.rem(me + k, n)}, device_id_type=MESH
        )
        return 0

    lax.fori_loop(1, n, greet, 0)

    row_l, col_l = iota((CHUNK, CHUNK), 0), iota((CHUNK, CHUNK), 1)
    token = token_of_row(row_l)
    lower = ones_where(col_l <= row_l)
    lower_p = ones_where(col_l <= token)
    perm[...] = ones_where(col_l == token)
    for k in range(3):
        cum_l[0:CHUNK, k * CHUNK : (k + 1) * CHUNK] = lower
        cum_l[CHUNK : 2 * CHUNK, k * CHUNK : (k + 1) * CHUNK] = lower_p
    head_dim_shift = (width // heads).bit_length() - 1
    expand[...] = ones_where(
        (iota((128, width), 0) & 63) == (iota((128, width), 1) >> head_dim_shift)
    )
    block_diag[...] = ones_where(
        (iota((LANES, LANES), 0) >> 6) == (iota((LANES, LANES), 1) >> 6)
    )
    state[...] = jnp.zeros_like(state)
    meta_s[...] = jnp.full(meta_s.shape, -1.0, F32)
    for copy in small:
        copy.wait()

    owners = o_v[...].astype(F32)
    meta_s[1:2, 0:frames] = owners
    owner_rows = jnp.broadcast_to(owners, (8, frames)).astype(BF16)
    spread = ones_where(
        iota((frames, frames * rows), 0) == (iota((frames, frames * rows), 1) >> 4)
    )
    owner_row = dot(owner_rows, spread)[0:1]
    shape = (n * rows, frames * rows)
    sel_s[...] = ones_where(
        ((iota(shape, 0) >> 4).astype(F32) == owner_row)
        & ((iota(shape, 0) & 15) == (iota(shape, 1) & 15))
    )

    def summarize(c, before):
        start = pl.multiple_of(c * CHUNK, CHUNK)
        decay = d_v[:, pl.ds(start, CHUNK)]
        high = decay.astype(BF16)
        left = decay - high.astype(F32)
        middle = left.astype(BF16)
        low = (left - middle.astype(F32)).astype(BF16)
        parts = jnp.concatenate([high, middle, low], axis=1)
        gap = jnp.zeros((64 - heads, parts.shape[1]), BF16)
        both = dot_t(cum_l[...], jnp.concatenate([parts, gap, parts, gap], axis=0))
        running, running_p = both[0:CHUNK], both[CHUNK : 2 * CHUNK]
        ref = running[CHUNK // 2 - 1 : CHUNK // 2]
        total = running[CHUNK - 1 : CHUNK]
        out_arg[c] = running_p - ref
        dev_arg[c] = running_p + before
        row = iota((16, 128), 0)
        extra = jnp.where(row == 0, ref, jnp.where(row == 1, total, total - ref))
        factors = two_parts(jnp.exp(jnp.concatenate([ref - running, extra], axis=0)))
        writes = w_v[:, pl.ds(start, CHUNK)]
        pltpu.make_async_copy(x_h.at[c], x_v.at[c], x_sem.at[c]).wait()
        for t in range(tiles):
            cols = slice(t * LANES, (t + 1) * LANES)
            full = dot(factors, expand[:, cols])
            scaled = (x_v[c, :, cols].astype(F32) * full[0:CHUNK]).astype(BF16)
            own = dot(writes, scaled)
            earlier = state[:, cols]
            xs_v[c, t, 0:CHUNK] = scaled
            xs_v[c, t, CHUNK : CHUNK + 64] = (earlier * full[CHUNK : CHUNK + 1]).astype(BF16)
            state[:, cols] = (
                earlier * full[CHUNK + 1 : CHUNK + 2] + own * full[CHUNK + 2 : CHUNK + 3]
            )
        return before + total

    total = lax.fori_loop(0, chunks, summarize, jnp.zeros((1, 128), F32))
    meta_s[0:1, :] = total
    for a in range(8):
        for b in range(4):
            send1[a * 4 + b] = state[8 * a : 8 * a + 8, 384 * b : 384 * b + 384].astype(BF16)

    pl.semaphore_wait(barrier, n - 1)

    def remote(source, target, sems, d):
        return pltpu.make_async_remote_copy(
            src_ref=source,
            dst_ref=target,
            send_sem=sems.at[0],
            recv_sem=sems.at[1],
            device_id={"span": d},
            device_id_type=MESH,
        )

    def all_of(ref, sem):
        part = ref.at[pl.ds(0, n - 1)]
        pltpu.make_async_copy(part, part, sem).wait()

    def send_meta(k, _):
        remote(meta_s, meta_r.at[me], meta_sem, lax.rem(me + k, n)).start()
        return 0

    lax.fori_loop(1, n, send_meta, 0)

    def send_one(k, _):
        d = lax.rem(me + k, n)
        remote(send1.at[d], recv1.at[me], one_sem, d).start()
        return 0

    lax.fori_loop(1, n, send_one, 0)
    meta_r[me] = meta_s[...]
    recv1[me] = send1[me]

    causal = iota((CHUNK, CHUNK), 1) <= token_of_row(iota((CHUNK, CHUNK), 0))

    def local(c, _):
        start = pl.multiple_of(c * CHUNK, CHUNK)
        reads = dot_t(perm[...], r_v[:, pl.ds(start, CHUNK)]).astype(BF16)
        rp_v[pl.ds(start, CHUNK), :] = reads
        scores = dot(reads, w_v[:, pl.ds(start, CHUNK)])
        masked = jnp.where(causal, scores, 0.0).astype(BF16)
        left = jnp.concatenate([masked, reads], axis=1)
        factors = two_parts(jnp.exp(jnp.concatenate([out_arg[c], dev_arg[c]], axis=0)))
        for t in range(tiles):
            full = dot(factors, expand[:, t * LANES : (t + 1) * LANES])
            mixed = dot(left, xs_v[c, t])
            ml_v[t, pl.ds(start, CHUNK), :] = mixed * full[0:CHUNK]
            od_v[t, pl.ds(start, CHUNK), :] = full[CHUNK : 2 * CHUNK]
        return 0

    lax.fori_loop(0, chunks, local, 0)

    all_of(meta_r, meta_sem.at[1])
    totals = meta_r[:, 0, :]
    factors = two_parts(jnp.exp(totals))
    for b in range(4):
        decays[b] = dot(factors, expand[:, 384 * b : 384 * b + 384])
    owned = jnp.max(jnp.where(meta_r[:, 1, :] == me.astype(F32), 1.0, 0.0), axis=1, keepdims=True)
    owned = jnp.broadcast_to(owned, (n, 128))
    rank = dot(ones_where(iota((n, n), 1) < iota((n, n), 0)), owned.astype(BF16))
    place = jnp.where(owned > 0.0, rank + 1.0, 0.0)[:, 0:1]
    shape = (n, n * rows)
    place_row = jnp.sum(
        jnp.where((iota(shape, 1) >> 4) == iota(shape, 0), place, 0.0), axis=0, keepdims=True
    )
    shape = (n * rows, n * rows)
    sel_r[...] = ones_where(
        (((iota(shape, 0) >> 4) + 1).astype(F32) == place_row)
        & ((iota(shape, 0) & 15) == (iota(shape, 1) & 15))
    )

    all_of(recv1, one_sem.at[1])
    quarter = lax.rem(me, 4)
    carry = jnp.zeros(recv1.shape[1:], F32)
    for i in range(n):
        send2[i] = carry.astype(BF16)
        if i < n - 1:
            carry = carry * decays[quarter, i : i + 1, :] + recv1[i].astype(F32)

    def send_two(k, _):
        d = lax.rem(me + k, n)
        remote(send2.at[d], recv2.at[me], two_sem, d).start()
        return 0

    lax.fori_loop(1, n, send_two, 0)
    recv2[me] = send2[me]
    all_of(recv2, two_sem.at[1])
    for a in range(8):
        for b in range(4):
            enter[8 * a : 8 * a + 8, 384 * b : 384 * b + 384] = recv2[a * 4 + b].astype(F32)

    def norm(t, _):
        first = pl.multiple_of(t * LANES, LANES)
        entering = enter[:, pl.ds(first, LANES)].astype(BF16)
        gain = jnp.concatenate([g_v[pl.ds(2 * t, 1), :], g_v[pl.ds(2 * t + 1, 1), :]], axis=1)
        for b in range(chunks // 2):
            part = slice(2 * b * CHUNK, 2 * (b + 1) * CHUNK)
            mixed = ml_v[t, part] + od_v[t, part] * dot(rp_v[part], entering)
            squares = dot((mixed * mixed).astype(BF16), block_diag[...])
            normed = mixed * lax.rsqrt(squares * (1.0 / GROUP) + EPSILON) * gain
            normed = normed.astype(BF16)
            for c in range(2):
                for q in range(4):
                    a_v[
                        (2 * b + c) * 32 : (2 * b + c + 1) * 32,
                        pl.ds(pl.multiple_of(q * width + t * LANES, LANES), LANES),
                    ] = normed[c * CHUNK + q * 32 : c * CHUNK + (q + 1) * 32]
        return 0

    lax.fori_loop(0, tiles, norm, 0)

    def deliver(t, _):
        pltpu.make_async_copy(
            wm_h.at[:, pl.ds(pl.multiple_of(t * LANES, LANES), LANES)], wm_v.at[t], wm_sem.at[t]
        ).wait()
        merged = dot(a_v[...], wm_v[t]).astype(BF16)
        send3[t] = dot(sel_s[...], merged).astype(BF16).reshape(n, rows, LANES)

        def send(k, _):
            d = lax.rem(me + k, n)
            pltpu.make_async_remote_copy(
                src_ref=send3.at[t, d],
                dst_ref=recv3.at[t, me],
                send_sem=del_s_sem,
                recv_sem=del_r_sem.at[t],
                device_id={"span": d},
                device_id_type=MESH,
            ).start()
            return 0

        lax.fori_loop(1, n, send, 0)
        recv3[t, me] = send3[t, me]
        return 0

    lax.fori_loop(0, tiles, deliver, 0)

    def arrive(t, _):
        part = recv3.at[t, pl.ds(0, n - 1)]
        pltpu.make_async_copy(part, part, del_r_sem.at[t]).wait()
        out_h[:, pl.ds(pl.multiple_of(t * LANES, LANES), LANES)] = dot(
            sel_r[...], recv3[t].reshape(n * rows, LANES)
        ).astype(BF16)
        return 0

    lax.fori_loop(0, tiles, arrive, 0)
    one_meta = meta_r.at[pl.ds(0, n - 1)]
    pltpu.make_async_copy(one_meta, one_meta, meta_sem.at[0]).wait()
    all_of(send1, one_sem.at[0])
    all_of(send2, two_sem.at[0])

    def sent(t, _):
        part = send3.at[t, pl.ds(0, n - 1)]
        pltpu.make_async_copy(part, part, del_s_sem).wait()
        return 0

    lax.fori_loop(0, tiles, sent, 0)


def shards(heads_in, writer, reader, log_decay, norm_gain, merge_weight, frame_owner):
    tokens, width = heads_in.shape
    n = lax.axis_size("span")
    chunks = tokens // CHUNK
    tiles = width // LANES
    frames = frame_owner.shape[0]
    state_size = writer.shape[1]
    deep, out_width = merge_weight.shape
    assert (n, state_size, width, out_width, frames) == (32, 64, 1536, 1536, 16)
    vmem, dma = pltpu.VMEM, pltpu.SemaphoreType.DMA
    in_place = pl.BlockSpec(memory_space=pltpu.HBM)
    return pl.pallas_call(
        functools.partial(kernel, n),
        out_shape=pltpu.VMEM((n * 16, out_width), BF16),
        in_specs=[in_place] * 7,
        out_specs=pl.BlockSpec(memory_space=pltpu.VMEM),
        scratch_shapes=[
            vmem((chunks, CHUNK, width), BF16),
            vmem(writer.shape[::-1], BF16),
            vmem(reader.shape[::-1], BF16),
            vmem(log_decay.shape[::-1], F32),
            vmem((width // 128, 128), F32),
            vmem((1, frames), jnp.int32),
            vmem((tiles, deep, LANES), BF16),
            vmem((2 * CHUNK, 3 * CHUNK), BF16),
            vmem((128, width), BF16),
            vmem((LANES, LANES), BF16),
            vmem((CHUNK, CHUNK), BF16),
            vmem((chunks, tiles, CHUNK + state_size, LANES), BF16),
            vmem((chunks, CHUNK, 128), F32),
            vmem((chunks, CHUNK, 128), F32),
            vmem((state_size, width), F32),
            vmem((tokens, state_size), BF16),
            vmem((tiles, tokens, LANES), F32),
            vmem((tiles, tokens, LANES), F32),
            vmem((tokens // 4, deep), BF16),
            vmem((8, 128), F32),
            vmem((n, 8, 128), F32),
            vmem((n, 8, 384), BF16),
            vmem((n, 8, 384), BF16),
            vmem((4, n, 384), F32),
            vmem((n, 8, 384), BF16),
            vmem((n, 8, 384), BF16),
            vmem((state_size, width), F32),
            vmem((n * 16, frames * 16), BF16),
            vmem((n * 16, n * 16), BF16),
            vmem((tiles, n, 16, LANES), BF16),
            vmem((tiles, n, 16, LANES), BF16),
            dma((chunks,)),
            dma((5,)),
            dma((tiles,)),
            dma((2,)),
            dma((2,)),
            dma((2,)),
            dma,
            dma((tiles,)),
        ],
        compiler_params=pltpu.CompilerParams(
            collective_id=0, has_side_effects=True, vmem_limit_bytes=52 * 1024 * 1024
        ),
    )(
        *(
            pltpu.with_memory_space_constraint(array, pltpu.HBM)
            for array in (
                heads_in.reshape(chunks, CHUNK, width),
                writer.T,
                reader.T,
                log_decay.T,
                norm_gain.reshape(width // 128, 128),
                frame_owner.reshape(1, frames),
                merge_weight,
            )
        )
    )


def solution(mesh):
    return jax.shard_map(
        shards,
        mesh=mesh,
        in_specs=(
            P(("batch", "span"), None),
            P(("batch", "span"), None),
            P(("batch", "span"), None),
            P(("batch", "span"), None),
            P(),
            P(),
            P(("batch", "span")),
        ),
        out_specs=P(("batch", "span"), None),
        check_vma=False,
    )
```

```python
import functools

import jax
import jax.numpy as jnp
from jax import lax
from jax.experimental import pallas as pl
from jax.experimental.pallas import tpu as pltpu
from jax.sharding import PartitionSpec as P

MESH = pl.DeviceIdType.MESH
F32 = jnp.float32
BF16 = jnp.bfloat16
EPSILON = 1e-05
FRAME_SIDE = 8
CHUNK = 128
LANES = 256
GROUP = 64


def dot(a, b):
    return lax.dot_general(a, b, (((1,), (0,)), ((), ())), preferred_element_type=F32)


def dot_t(a, b):
    return lax.dot_general(a, b, (((1,), (1,)), ((), ())), preferred_element_type=F32)


def iota(shape, axis):
    return lax.broadcasted_iota(jnp.int32, shape, axis)


def ones_where(condition):
    return jnp.where(condition, 1.0, 0.0).astype(BF16)


def token_of_row(row):
    q, rest = row >> 5, row & 31
    frame, i2, j2 = rest >> 4, (rest >> 2) & 3, rest & 3
    return frame * 64 + (2 * i2 + (q >> 1)) * 8 + 2 * j2 + (q & 1)


def two_parts(values):
    high = values.astype(BF16)
    low = (values - high.astype(F32)).astype(BF16)
    return jnp.where(iota(values.shape, 1) < 64, high.astype(F32), low.astype(F32)).astype(BF16)


def kernel(
    n, x_h, w_h, r_h, d_h, g_h, o_h, wm_h, out_h,
    x_v, w_v, r_v, d_v, g_v, o_v, wm_v,
    cum_l, expand, block_diag, perm, xs_v, in_factor, out_arg, out_factor, left_v, state, rp_v, ml_v, od_v, a_v,
    meta_s, meta_r, send1, recv1, decays, send2, recv2, enter, sel_s, sel_r, send3, recv3,
    x_sem, in_sem, wm_sem, meta_sem, one_sem, two_sem, del_s_sem, del_r_sem,
):
    me = lax.axis_index("span")
    tokens, width = x_h.shape
    chunks = tokens // CHUNK
    heads = d_h.shape[0]
    tiles = width // LANES
    frames = o_h.shape[1]
    rows = 16

    small = [
        pltpu.make_async_copy(s, d, in_sem.at[k])
        for k, (s, d) in enumerate(((d_h, d_v), (w_h, w_v), (r_h, r_v), (g_h, g_v), (o_h, o_v)))
    ]

    def columns(t):
        return pl.ds(pl.multiple_of(t * LANES, LANES), LANES)

    def load(t):
        return pltpu.make_async_copy(x_h.at[:, columns(t)], x_v.at[t], x_sem.at[t])

    def load_weight(t):
        return pltpu.make_async_copy(wm_h.at[:, columns(t)], wm_v.at[t], wm_sem.at[t])

    for copy in small + [load(t) for t in range(tiles)]:
        copy.start()

    barrier = pltpu.get_barrier_semaphore()

    def greet(k, _):
        pl.semaphore_signal(
            barrier, inc=1, device_id={"span": lax.rem(me + k, n)}, device_id_type=MESH
        )
        return 0

    lax.fori_loop(1, n, greet, 0)

    row_l, col_l = iota((CHUNK, CHUNK), 0), iota((CHUNK, CHUNK), 1)
    token = token_of_row(row_l)
    lower = ones_where(col_l <= row_l)
    lower_p = ones_where(col_l <= token)
    perm[...] = ones_where(col_l == token)
    for k in range(3):
        cum_l[0:CHUNK, k * CHUNK : (k + 1) * CHUNK] = lower
        cum_l[CHUNK : 2 * CHUNK, k * CHUNK : (k + 1) * CHUNK] = lower_p
    head_dim_shift = (width // heads).bit_length() - 1
    expand[...] = ones_where(
        (iota((128, width), 0) & 63) == (iota((128, width), 1) >> head_dim_shift)
    )
    block_diag[...] = jnp.where(
        (iota((LANES, LANES), 0) >> 6) == (iota((LANES, LANES), 1) >> 6), 1.0 / GROUP, 0.0
    ).astype(BF16)
    meta_s[...] = jnp.full(meta_s.shape, -1.0, F32)
    for copy in small:
        copy.wait()

    owners = o_v[...].astype(F32)
    meta_s[1:2, 0:frames] = owners
    owner_rows = jnp.broadcast_to(owners, (8, frames)).astype(BF16)
    spread = ones_where(
        iota((frames, frames * rows), 0) == (iota((frames, frames * rows), 1) >> 4)
    )
    owner_row = dot(owner_rows, spread)[0:1]
    shape = (n * rows, frames * rows)
    sel_s[...] = ones_where(
        ((iota(shape, 0) >> 4).astype(F32) == owner_row)
        & ((iota(shape, 0) & 15) == (iota(shape, 1) & 15))
    )

    before = jnp.zeros((1, 128), F32)
    for c in range(chunks):
        part = slice(c * CHUNK, (c + 1) * CHUNK)
        decay = d_v[:, part]
        high = decay.astype(BF16)
        left = decay - high.astype(F32)
        middle = left.astype(BF16)
        low = (left - middle.astype(F32)).astype(BF16)
        parts = jnp.concatenate([high, middle, low], axis=1)
        gap = jnp.zeros((64 - heads, parts.shape[1]), BF16)
        both = dot_t(cum_l[...], jnp.concatenate([parts, gap, parts, gap], axis=0))
        running, running_p = both[0:CHUNK], both[CHUNK : 2 * CHUNK]
        ref = running[CHUNK // 2 - 1 : CHUNK // 2]
        total = running[CHUNK - 1 : CHUNK]
        out_arg[c, 0:CHUNK] = running_p - ref
        out_arg[c, CHUNK : 2 * CHUNK] = running_p + before
        row = iota((16, 128), 0)
        extra = jnp.where(row == 0, ref, jnp.where(row == 1, total, total - ref))
        in_factor[c] = two_parts(jnp.exp(jnp.concatenate([ref - running, extra], axis=0)))
        before = before + total
    meta_s[0:1, :] = before

    def summarize(t, _):
        load(t).wait()
        spread = expand[:, columns(t)]
        carry = jnp.zeros((w_v.shape[0], LANES), F32)
        for c in range(chunks):
            part = slice(c * CHUNK, (c + 1) * CHUNK)
            full = dot(in_factor[c], spread)
            scaled = (x_v[t, part].astype(F32) * full[0:CHUNK]).astype(BF16)
            own = dot(w_v[:, part], scaled)
            xs_v[c, t, 0:CHUNK] = scaled
            xs_v[c, t, CHUNK : CHUNK + 64] = (carry * full[CHUNK : CHUNK + 1]).astype(BF16)
            carry = carry * full[CHUNK + 1 : CHUNK + 2] + own * full[CHUNK + 2 : CHUNK + 3]
        state[:, columns(t)] = carry
        return 0

    lax.fori_loop(0, tiles, summarize, 0)
    for a in range(8):
        for b in range(4):
            send1[a * 4 + b] = state[8 * a : 8 * a + 8, 384 * b : 384 * b + 384].astype(BF16)

    pl.semaphore_wait(barrier, n - 1)

    def remote(source, target, sems, d):
        return pltpu.make_async_remote_copy(
            src_ref=source,
            dst_ref=target,
            send_sem=sems.at[0],
            recv_sem=sems.at[1],
            device_id={"span": d},
            device_id_type=MESH,
        )

    def all_of(ref, sem):
        part = ref.at[pl.ds(0, n - 1)]
        pltpu.make_async_copy(part, part, sem).wait()

    def send_meta(k, _):
        remote(meta_s, meta_r.at[me], meta_sem, lax.rem(me + k, n)).start()
        return 0

    lax.fori_loop(1, n, send_meta, 0)

    def send_one(k, _):
        d = lax.rem(me + k, n)
        remote(send1.at[d], recv1.at[me], one_sem, d).start()
        return 0

    lax.fori_loop(1, n, send_one, 0)
    for t in range(tiles):
        load_weight(t).start()
    meta_r[me] = meta_s[...]
    recv1[me] = send1[me]

    causal = iota((CHUNK, CHUNK), 1) <= token_of_row(iota((CHUNK, CHUNK), 0))

    for c in range(chunks):
        part = slice(c * CHUNK, (c + 1) * CHUNK)
        reads = dot_t(perm[...], r_v[:, part]).astype(BF16)
        scores = dot(reads, w_v[:, part])
        rp_v[part] = reads
        left_v[c] = jnp.concatenate([jnp.where(causal, scores, 0.0).astype(BF16), reads], axis=1)
        out_factor[c] = two_parts(jnp.exp(out_arg[c]))

    def local(t, _):
        spread = expand[:, columns(t)]
        for c in range(chunks):
            part = slice(c * CHUNK, (c + 1) * CHUNK)
            full = dot(out_factor[c], spread)
            ml_v[t, part] = dot(left_v[c], xs_v[c, t]) * full[0:CHUNK]
            od_v[t, part] = full[CHUNK : 2 * CHUNK]
        return 0

    lax.fori_loop(0, tiles // 2, local, 0)

    all_of(meta_r, meta_sem.at[1])
    totals = meta_r[:, 0, :]
    factors = two_parts(jnp.exp(totals))
    for b in range(4):
        decays[b] = dot(factors, expand[:, 384 * b : 384 * b + 384])
    all_of(recv1, one_sem.at[1])
    quarter = lax.rem(me, 4)
    carry = jnp.zeros(recv1.shape[1:], F32)
    for i in range(n):
        send2[i] = carry.astype(BF16)
        if i < n - 1:
            carry = carry * decays[quarter, i : i + 1, :] + recv1[i].astype(F32)

    def send_two(k, _):
        d = lax.rem(me + k, n)
        remote(send2.at[d], recv2.at[me], two_sem, d).start()
        return 0

    lax.fori_loop(1, n, send_two, 0)
    recv2[me] = send2[me]
    lax.fori_loop(tiles // 2, tiles, local, 0)
    owned = jnp.max(jnp.where(meta_r[:, 1, :] == me.astype(F32), 1.0, 0.0), axis=1, keepdims=True)
    owned = jnp.broadcast_to(owned, (n, 128))
    rank = dot(ones_where(iota((n, n), 1) < iota((n, n), 0)), owned.astype(BF16))
    place = jnp.where(owned > 0.0, rank + 1.0, 0.0)[:, 0:1]
    shape = (n, n * rows)
    place_row = jnp.sum(
        jnp.where((iota(shape, 1) >> 4) == iota(shape, 0), place, 0.0), axis=0, keepdims=True
    )
    shape = (n * rows, n * rows)
    sel_r[...] = ones_where(
        (((iota(shape, 0) >> 4) + 1).astype(F32) == place_row)
        & ((iota(shape, 0) & 15) == (iota(shape, 1) & 15))
    )

    all_of(recv2, two_sem.at[1])
    for a in range(8):
        for b in range(4):
            enter[8 * a : 8 * a + 8, 384 * b : 384 * b + 384] = recv2[a * 4 + b].astype(F32)

    def norm(t, _):
        entering = enter[:, columns(t)].astype(BF16)
        gain = jnp.concatenate([g_v[pl.ds(2 * t, 1), :], g_v[pl.ds(2 * t + 1, 1), :]], axis=1)
        for b in range(chunks // 2):
            part = slice(2 * b * CHUNK, 2 * (b + 1) * CHUNK)
            mixed = ml_v[t, part] + od_v[t, part] * dot(rp_v[part], entering)
            squares = dot((mixed * mixed).astype(BF16), block_diag[...])
            normed = mixed * lax.rsqrt(squares + EPSILON) * gain
            normed = normed.astype(BF16)
            for c in range(2):
                for q in range(4):
                    a_v[
                        (2 * b + c) * 32 : (2 * b + c + 1) * 32,
                        pl.ds(pl.multiple_of(q * width + t * LANES, LANES), LANES),
                    ] = normed[c * CHUNK + q * 32 : c * CHUNK + (q + 1) * 32]
        return 0

    lax.fori_loop(0, tiles, norm, 0)

    def deliver(t, _):
        load_weight(t).wait()
        merged = dot(a_v[...], wm_v[t]).astype(BF16)
        send3[t] = dot(sel_s[...], merged).astype(BF16).reshape(n, rows, LANES)

        def send(k, _):
            d = lax.rem(me + k, n)
            pltpu.make_async_remote_copy(
                src_ref=send3.at[t, d],
                dst_ref=recv3.at[t, me],
                send_sem=del_s_sem,
                recv_sem=del_r_sem.at[t],
                device_id={"span": d},
                device_id_type=MESH,
            ).start()
            return 0

        lax.fori_loop(1, n, send, 0)
        recv3[t, me] = send3[t, me]
        return 0

    lax.fori_loop(0, tiles, deliver, 0)

    def arrive(t, _):
        part = recv3.at[t, pl.ds(0, n - 1)]
        pltpu.make_async_copy(part, part, del_r_sem.at[t]).wait()
        out_h[:, columns(t)] = dot(
            sel_r[...], recv3[t].reshape(n * rows, LANES)
        ).astype(BF16)
        return 0

    lax.fori_loop(0, tiles, arrive, 0)
    one_meta = meta_r.at[pl.ds(0, n - 1)]
    pltpu.make_async_copy(one_meta, one_meta, meta_sem.at[0]).wait()
    all_of(send1, one_sem.at[0])
    all_of(send2, two_sem.at[0])

    def sent(t, _):
        part = send3.at[t, pl.ds(0, n - 1)]
        pltpu.make_async_copy(part, part, del_s_sem).wait()
        return 0

    lax.fori_loop(0, tiles, sent, 0)


def shards(heads_in, writer, reader, log_decay, norm_gain, merge_weight, frame_owner):
    tokens, width = heads_in.shape
    n = lax.axis_size("span")
    chunks = tokens // CHUNK
    tiles = width // LANES
    frames = frame_owner.shape[0]
    state_size = writer.shape[1]
    deep, out_width = merge_weight.shape
    assert (n, state_size, width, out_width, frames) == (32, 64, 1536, 1536, 16)
    vmem, dma = pltpu.VMEM, pltpu.SemaphoreType.DMA
    in_place = pl.BlockSpec(memory_space=pltpu.HBM)
    return pl.pallas_call(
        functools.partial(kernel, n),
        out_shape=pltpu.VMEM((n * 16, out_width), BF16),
        in_specs=[in_place] * 7,
        out_specs=pl.BlockSpec(memory_space=pltpu.VMEM),
        scratch_shapes=[
            vmem((tiles, tokens, LANES), BF16),
            vmem(writer.shape[::-1], BF16),
            vmem(reader.shape[::-1], BF16),
            vmem(log_decay.shape[::-1], F32),
            vmem((width // 128, 128), F32),
            vmem((1, frames), jnp.int32),
            vmem((tiles, deep, LANES), BF16),
            vmem((2 * CHUNK, 3 * CHUNK), BF16),
            vmem((128, width), BF16),
            vmem((LANES, LANES), BF16),
            vmem((CHUNK, CHUNK), BF16),
            vmem((chunks, tiles, CHUNK + state_size, LANES), BF16),
            vmem((chunks, CHUNK + 16, 128), BF16),
            vmem((chunks, 2 * CHUNK, 128), F32),
            vmem((chunks, 2 * CHUNK, 128), BF16),
            vmem((chunks, CHUNK, CHUNK + state_size), BF16),
            vmem((state_size, width), F32),
            vmem((tokens, state_size), BF16),
            vmem((tiles, tokens, LANES), F32),
            vmem((tiles, tokens, LANES), F32),
            vmem((tokens // 4, deep), BF16),
            vmem((8, 128), F32),
            vmem((n, 8, 128), F32),
            vmem((n, 8, 384), BF16),
            vmem((n, 8, 384), BF16),
            vmem((4, n, 384), F32),
            vmem((n, 8, 384), BF16),
            vmem((n, 8, 384), BF16),
            vmem((state_size, width), F32),
            vmem((n * 16, frames * 16), BF16),
            vmem((n * 16, n * 16), BF16),
            vmem((tiles, n, 16, LANES), BF16),
            vmem((tiles, n, 16, LANES), BF16),
            dma((tiles,)),
            dma((5,)),
            dma((tiles,)),
            dma((2,)),
            dma((2,)),
            dma((2,)),
            dma,
            dma((tiles,)),
        ],
        compiler_params=pltpu.CompilerParams(
            collective_id=0, has_side_effects=True, vmem_limit_bytes=52 * 1024 * 1024
        ),
    )(
        *(
            pltpu.with_memory_space_constraint(array, pltpu.HBM)
            for array in (
                heads_in,
                writer.T,
                reader.T,
                log_decay.T,
                norm_gain.reshape(width // 128, 128),
                frame_owner.reshape(1, frames),
                merge_weight,
            )
        )
    )


def solution(mesh):
    return jax.shard_map(
        shards,
        mesh=mesh,
        in_specs=(
            P(("batch", "span"), None),
            P(("batch", "span"), None),
            P(("batch", "span"), None),
            P(("batch", "span"), None),
            P(),
            P(),
            P(("batch", "span")),
        ),
        out_specs=P(("batch", "span"), None),
        check_vma=False,
    )
```

```python
import functools

import jax
import jax.numpy as jnp
from jax import lax
from jax.experimental import pallas as pl
from jax.experimental.pallas import tpu as pltpu
from jax.sharding import PartitionSpec as P

MESH = pl.DeviceIdType.MESH
F32 = jnp.float32
BF16 = jnp.bfloat16
EPSILON = 1e-05
FRAME_SIDE = 8
CHUNK = 128
LANES = 256
GROUP = 64


def dot(a, b):
    return lax.dot_general(a, b, (((1,), (0,)), ((), ())), preferred_element_type=F32)


def dot_t(a, b):
    return lax.dot_general(a, b, (((1,), (1,)), ((), ())), preferred_element_type=F32)


def iota(shape, axis):
    return lax.broadcasted_iota(jnp.int32, shape, axis)


def ones_where(condition):
    return jnp.where(condition, 1.0, 0.0).astype(BF16)


def token_of_row(row):
    q, rest = row >> 5, row & 31
    frame, i2, j2 = rest >> 4, (rest >> 2) & 3, rest & 3
    return frame * 64 + (2 * i2 + (q >> 1)) * 8 + 2 * j2 + (q & 1)


def two_parts(values):
    high = values.astype(BF16)
    low = (values - high.astype(F32)).astype(BF16)
    return jnp.where(iota(values.shape, 1) < 64, high.astype(F32), low.astype(F32)).astype(BF16)


def kernel(
    n, x_h, w_h, r_h, d_h, g_h, o_h, wm_h, out_h,
    x_v, w_v, r_v, d_v, g_v, o_v, wm_v,
    cum_l, expand, block_diag, perm, xs_v, in_factor, out_arg, out_factor, left_v, state, rp_v, ml_v, od_v, a_v,
    meta_s, meta_r, send1, recv1, decays, send2, recv2, enter, sel_s, sel_r, send3, recv3,
    x_sem, in_sem, wm_sem, meta_sem, one_sem, two_sem, del_s_sem, del_r_sem,
):
    me = lax.axis_index("span")
    tokens, width = x_h.shape
    chunks = tokens // CHUNK
    heads = d_h.shape[0]
    tiles = width // LANES
    frames = o_h.shape[1]
    rows = 16

    small = [
        pltpu.make_async_copy(s, d, in_sem.at[k])
        for k, (s, d) in enumerate(((d_h, d_v), (w_h, w_v), (r_h, r_v), (g_h, g_v), (o_h, o_v)))
    ]

    def columns(t):
        return pl.ds(pl.multiple_of(t * LANES, LANES), LANES)

    def load(t):
        return pltpu.make_async_copy(x_h.at[:, columns(t)], x_v.at[t], x_sem.at[t])

    def load_weight(t):
        return pltpu.make_async_copy(wm_h.at[:, columns(t)], wm_v.at[t], wm_sem.at[t])

    for copy in small + [load(t) for t in range(tiles)]:
        copy.start()

    barrier = pltpu.get_barrier_semaphore()

    def greet(k, _):
        pl.semaphore_signal(
            barrier, inc=1, device_id={"span": lax.rem(me + k, n)}, device_id_type=MESH
        )
        return 0

    lax.fori_loop(1, n, greet, 0)

    row_l, col_l = iota((CHUNK, CHUNK), 0), iota((CHUNK, CHUNK), 1)
    token = token_of_row(row_l)
    lower = ones_where(col_l <= row_l)
    lower_p = ones_where(col_l <= token)
    perm[...] = ones_where(col_l == token)
    for k in range(3):
        cum_l[0:CHUNK, k * CHUNK : (k + 1) * CHUNK] = lower
        cum_l[CHUNK : 2 * CHUNK, k * CHUNK : (k + 1) * CHUNK] = lower_p
    head_dim_shift = (width // heads).bit_length() - 1
    expand[...] = ones_where(
        (iota((128, width), 0) & 63) == (iota((128, width), 1) >> head_dim_shift)
    )
    block_diag[...] = jnp.where(
        (iota((LANES, LANES), 0) >> 6) == (iota((LANES, LANES), 1) >> 6), 1.0 / GROUP, 0.0
    ).astype(BF16)
    meta_s[...] = jnp.full(meta_s.shape, -1.0, F32)
    for copy in small:
        copy.wait()

    owners = o_v[...].astype(F32)
    meta_s[1:2, 0:frames] = owners
    owner_rows = jnp.broadcast_to(owners, (8, frames)).astype(BF16)
    spread = ones_where(
        iota((frames, frames * rows), 0) == (iota((frames, frames * rows), 1) >> 4)
    )
    owner_row = dot(owner_rows, spread)[0:1]
    shape = (n * rows, frames * rows)
    sel_s[...] = ones_where(
        ((iota(shape, 0) >> 4).astype(F32) == owner_row)
        & ((iota(shape, 0) & 15) == (iota(shape, 1) & 15))
    )

    before = jnp.zeros((1, 128), F32)
    for c in range(chunks):
        part = slice(c * CHUNK, (c + 1) * CHUNK)
        decay = d_v[:, part]
        high = decay.astype(BF16)
        left = decay - high.astype(F32)
        middle = left.astype(BF16)
        low = (left - middle.astype(F32)).astype(BF16)
        parts = jnp.concatenate([high, middle, low], axis=1)
        gap = jnp.zeros((64 - heads, parts.shape[1]), BF16)
        both = dot_t(cum_l[...], jnp.concatenate([parts, gap, parts, gap], axis=0))
        running, running_p = both[0:CHUNK], both[CHUNK : 2 * CHUNK]
        ref = running[CHUNK // 2 - 1 : CHUNK // 2]
        total = running[CHUNK - 1 : CHUNK]
        out_arg[c, 0:CHUNK] = running_p - ref
        out_arg[c, CHUNK : 2 * CHUNK] = running_p + before
        row = iota((16, 128), 0)
        extra = jnp.where(row == 0, ref, jnp.where(row == 1, total, total - ref))
        in_factor[c] = two_parts(jnp.exp(jnp.concatenate([ref - running, extra], axis=0)))
        before = before + total
    meta_s[0:1, :] = before

    def summarize(t, _):
        load(t).wait()
        spread = expand[:, columns(t)]
        carry = jnp.zeros((w_v.shape[0], LANES), F32)
        full, scaled = {}, {}
        for k in range(chunks + 2):
            if k < chunks:
                full[k] = dot(in_factor[k], spread)
            c = k - 1
            if 0 <= c < chunks:
                part = slice(c * CHUNK, (c + 1) * CHUNK)
                scaled[c] = (x_v[t, part].astype(F32) * full[c][0:CHUNK]).astype(BF16)
                xs_v[c, t, 0:CHUNK] = scaled[c]
            c = k - 2
            if c >= 0:
                own = dot(w_v[:, c * CHUNK : (c + 1) * CHUNK], scaled.pop(c))
                scales = full.pop(c)[CHUNK : CHUNK + 3]
                xs_v[c, t, CHUNK : CHUNK + 64] = (carry * scales[0:1]).astype(BF16)
                carry = carry * scales[1:2] + own * scales[2:3]
        state[:, columns(t)] = carry
        return 0

    lax.fori_loop(0, tiles, summarize, 0)
    for a in range(8):
        for b in range(4):
            send1[a * 4 + b] = state[8 * a : 8 * a + 8, 384 * b : 384 * b + 384].astype(BF16)

    pl.semaphore_wait(barrier, n - 1)

    def remote(source, target, sems, d):
        return pltpu.make_async_remote_copy(
            src_ref=source,
            dst_ref=target,
            send_sem=sems.at[0],
            recv_sem=sems.at[1],
            device_id={"span": d},
            device_id_type=MESH,
        )

    def all_of(ref, sem):
        part = ref.at[pl.ds(0, n - 1)]
        pltpu.make_async_copy(part, part, sem).wait()

    def send_meta(k, _):
        remote(meta_s, meta_r.at[me], meta_sem, lax.rem(me + k, n)).start()
        return 0

    lax.fori_loop(1, n, send_meta, 0)

    def send_one(k, _):
        d = lax.rem(me + k, n)
        remote(send1.at[d], recv1.at[me], one_sem, d).start()
        return 0

    lax.fori_loop(1, n, send_one, 0)
    for t in range(tiles):
        load_weight(t).start()
    meta_r[me] = meta_s[...]
    recv1[me] = send1[me]

    causal = iota((CHUNK, CHUNK), 1) <= token_of_row(iota((CHUNK, CHUNK), 0))

    for c in range(chunks):
        part = slice(c * CHUNK, (c + 1) * CHUNK)
        reads = dot_t(perm[...], r_v[:, part]).astype(BF16)
        scores = dot(reads, w_v[:, part])
        rp_v[part] = reads
        left_v[c] = jnp.concatenate([jnp.where(causal, scores, 0.0).astype(BF16), reads], axis=1)
        out_factor[c] = two_parts(jnp.exp(out_arg[c]))

    def local(t, _):
        spread = expand[:, columns(t)]
        for c in range(chunks):
            part = slice(c * CHUNK, (c + 1) * CHUNK)
            full = dot(out_factor[c], spread)
            ml_v[t, part] = dot(left_v[c], xs_v[c, t]) * full[0:CHUNK]
            od_v[t, part] = full[CHUNK : 2 * CHUNK]
        return 0

    lax.fori_loop(0, tiles // 2, local, 0)

    all_of(meta_r, meta_sem.at[1])
    totals = meta_r[:, 0, :]
    factors = two_parts(jnp.exp(totals))
    for b in range(4):
        decays[b] = dot(factors, expand[:, 384 * b : 384 * b + 384])
    all_of(recv1, one_sem.at[1])
    quarter = lax.rem(me, 4)
    carry = jnp.zeros(recv1.shape[1:], F32)
    for i in range(n):
        send2[i] = carry.astype(BF16)
        if i < n - 1:
            carry = carry * decays[quarter, i : i + 1, :] + recv1[i].astype(F32)

    def send_two(k, _):
        d = lax.rem(me + k, n)
        remote(send2.at[d], recv2.at[me], two_sem, d).start()
        return 0

    lax.fori_loop(1, n, send_two, 0)
    recv2[me] = send2[me]
    lax.fori_loop(tiles // 2, tiles, local, 0)
    owned = jnp.max(jnp.where(meta_r[:, 1, :] == me.astype(F32), 1.0, 0.0), axis=1, keepdims=True)
    owned = jnp.broadcast_to(owned, (n, 128))
    rank = dot(ones_where(iota((n, n), 1) < iota((n, n), 0)), owned.astype(BF16))
    place = jnp.where(owned > 0.0, rank + 1.0, 0.0)[:, 0:1]
    shape = (n, n * rows)
    place_row = jnp.sum(
        jnp.where((iota(shape, 1) >> 4) == iota(shape, 0), place, 0.0), axis=0, keepdims=True
    )
    shape = (n * rows, n * rows)
    sel_r[...] = ones_where(
        (((iota(shape, 0) >> 4) + 1).astype(F32) == place_row)
        & ((iota(shape, 0) & 15) == (iota(shape, 1) & 15))
    )

    all_of(recv2, two_sem.at[1])
    for a in range(8):
        for b in range(4):
            enter[8 * a : 8 * a + 8, 384 * b : 384 * b + 384] = recv2[a * 4 + b].astype(F32)

    def norm(t, _):
        entering = enter[:, columns(t)].astype(BF16)
        gain = jnp.concatenate([g_v[pl.ds(2 * t, 1), :], g_v[pl.ds(2 * t + 1, 1), :]], axis=1)
        mixed, squares = {}, {}
        for k in range(chunks + 2):
            if k < chunks:
                part = slice(k * CHUNK, (k + 1) * CHUNK)
                mixed[k] = ml_v[t, part] + od_v[t, part] * dot(rp_v[part], entering)
            c = k - 1
            if 0 <= c < chunks:
                squares[c] = dot((mixed[c] * mixed[c]).astype(BF16), block_diag[...])
            c = k - 2
            if c >= 0:
                normed = mixed.pop(c) * lax.rsqrt(squares.pop(c) + EPSILON) * gain
                normed = normed.astype(BF16)
                for q in range(4):
                    first = pl.multiple_of(q * width + t * LANES, LANES)
                    a_v[c * 32 : (c + 1) * 32, pl.ds(first, LANES)] = normed[q * 32 : (q + 1) * 32]
        return 0

    lax.fori_loop(0, tiles, norm, 0)

    def deliver(t, _):
        load_weight(t).wait()
        merged = dot(a_v[...], wm_v[t]).astype(BF16)
        send3[t] = dot(sel_s[...], merged).astype(BF16).reshape(n, rows, LANES)

        def send(k, _):
            d = lax.rem(me + k, n)
            pltpu.make_async_remote_copy(
                src_ref=send3.at[t, d],
                dst_ref=recv3.at[t, me],
                send_sem=del_s_sem,
                recv_sem=del_r_sem.at[t],
                device_id={"span": d},
                device_id_type=MESH,
            ).start()
            return 0

        lax.fori_loop(1, n, send, 0)
        recv3[t, me] = send3[t, me]
        return 0

    lax.fori_loop(0, tiles, deliver, 0)

    def arrive(t, _):
        part = recv3.at[t, pl.ds(0, n - 1)]
        pltpu.make_async_copy(part, part, del_r_sem.at[t]).wait()
        out_h[:, columns(t)] = dot(
            sel_r[...], recv3[t].reshape(n * rows, LANES)
        ).astype(BF16)
        return 0

    lax.fori_loop(0, tiles, arrive, 0)
    one_meta = meta_r.at[pl.ds(0, n - 1)]
    pltpu.make_async_copy(one_meta, one_meta, meta_sem.at[0]).wait()
    all_of(send1, one_sem.at[0])
    all_of(send2, two_sem.at[0])

    def sent(t, _):
        part = send3.at[t, pl.ds(0, n - 1)]
        pltpu.make_async_copy(part, part, del_s_sem).wait()
        return 0

    lax.fori_loop(0, tiles, sent, 0)


def shards(heads_in, writer, reader, log_decay, norm_gain, merge_weight, frame_owner):
    tokens, width = heads_in.shape
    n = lax.axis_size("span")
    chunks = tokens // CHUNK
    tiles = width // LANES
    frames = frame_owner.shape[0]
    state_size = writer.shape[1]
    deep, out_width = merge_weight.shape
    assert (n, state_size, width, out_width, frames) == (32, 64, 1536, 1536, 16)
    vmem, dma = pltpu.VMEM, pltpu.SemaphoreType.DMA
    in_place = pl.BlockSpec(memory_space=pltpu.HBM)
    return pl.pallas_call(
        functools.partial(kernel, n),
        out_shape=pltpu.VMEM((n * 16, out_width), BF16),
        in_specs=[in_place] * 7,
        out_specs=pl.BlockSpec(memory_space=pltpu.VMEM),
        scratch_shapes=[
            vmem((tiles, tokens, LANES), BF16),
            vmem(writer.shape[::-1], BF16),
            vmem(reader.shape[::-1], BF16),
            vmem(log_decay.shape[::-1], F32),
            vmem((width // 128, 128), F32),
            vmem((1, frames), jnp.int32),
            vmem((tiles, deep, LANES), BF16),
            vmem((2 * CHUNK, 3 * CHUNK), BF16),
            vmem((128, width), BF16),
            vmem((LANES, LANES), BF16),
            vmem((CHUNK, CHUNK), BF16),
            vmem((chunks, tiles, CHUNK + state_size, LANES), BF16),
            vmem((chunks, CHUNK + 16, 128), BF16),
            vmem((chunks, 2 * CHUNK, 128), F32),
            vmem((chunks, 2 * CHUNK, 128), BF16),
            vmem((chunks, CHUNK, CHUNK + state_size), BF16),
            vmem((state_size, width), F32),
            vmem((tokens, state_size), BF16),
            vmem((tiles, tokens, LANES), F32),
            vmem((tiles, tokens, LANES), F32),
            vmem((tokens // 4, deep), BF16),
            vmem((8, 128), F32),
            vmem((n, 8, 128), F32),
            vmem((n, 8, 384), BF16),
            vmem((n, 8, 384), BF16),
            vmem((4, n, 384), F32),
            vmem((n, 8, 384), BF16),
            vmem((n, 8, 384), BF16),
            vmem((state_size, width), F32),
            vmem((n * 16, frames * 16), BF16),
            vmem((n * 16, n * 16), BF16),
            vmem((tiles, n, 16, LANES), BF16),
            vmem((tiles, n, 16, LANES), BF16),
            dma((tiles,)),
            dma((5,)),
            dma((tiles,)),
            dma((2,)),
            dma((2,)),
            dma((2,)),
            dma,
            dma((tiles,)),
        ],
        compiler_params=pltpu.CompilerParams(
            collective_id=0, has_side_effects=True, vmem_limit_bytes=52 * 1024 * 1024
        ),
    )(
        *(
            pltpu.with_memory_space_constraint(array, pltpu.HBM)
            for array in (
                heads_in,
                writer.T,
                reader.T,
                log_decay.T,
                norm_gain.reshape(width // 128, 128),
                frame_owner.reshape(1, frames),
                merge_weight,
            )
        )
    )


def solution(mesh):
    return jax.shard_map(
        shards,
        mesh=mesh,
        in_specs=(
            P(("batch", "span"), None),
            P(("batch", "span"), None),
            P(("batch", "span"), None),
            P(("batch", "span"), None),
            P(),
            P(),
            P(("batch", "span")),
        ),
        out_specs=P(("batch", "span"), None),
        check_vma=False,
    )
```

```python
import functools

import jax
import jax.numpy as jnp
from jax import lax
from jax.experimental import pallas as pl
from jax.experimental.pallas import tpu as pltpu
from jax.sharding import PartitionSpec as P

MESH = pl.DeviceIdType.MESH
F32 = jnp.float32
BF16 = jnp.bfloat16
EPSILON = 1e-05
FRAME_SIDE = 8
CHUNK = 128
LANES = 256
GROUP = 64


def dot(a, b):
    return lax.dot_general(a, b, (((1,), (0,)), ((), ())), preferred_element_type=F32)


def dot_t(a, b):
    return lax.dot_general(a, b, (((1,), (1,)), ((), ())), preferred_element_type=F32)


def iota(shape, axis):
    return lax.broadcasted_iota(jnp.int32, shape, axis)


def ones_where(condition):
    return jnp.where(condition, 1.0, 0.0).astype(BF16)


def slice_of(p):
    b = (p & 1) * 2 + ((p >> 1) & 1)
    return slice(8 * (p >> 2), 8 * (p >> 2) + 8), slice(384 * b, 384 * b + 384)


def token_of_row(row):
    q, rest = row >> 5, row & 31
    frame, i2, j2 = rest >> 4, (rest >> 2) & 3, rest & 3
    return frame * 64 + (2 * i2 + (q >> 1)) * 8 + 2 * j2 + (q & 1)


def two_parts(values):
    high = values.astype(BF16)
    low = (values - high.astype(F32)).astype(BF16)
    return jnp.where(iota(values.shape, 1) < 64, high.astype(F32), low.astype(F32)).astype(BF16)


def kernel(
    n, x_h, w_h, r_h, d_h, g_h, o_h, wm_h, out_h,
    x_v, w_v, r_v, d_v, g_v, o_v, wm_v,
    cum_l, expand, block_diag, xs_v, in_factor, out_arg, out_factor, left_v, state, rp_v, ml_v, od_v, a_v,
    meta_s, meta_r, send1, recv1, decays, send2, recv2, enter, sel_s, sel_r, send3, recv3,
    x_sem, in_sem, wm_sem, meta_sem, one_sem, two_sem, del_s_sem, del_r_sem,
):
    me = lax.axis_index("span")
    tokens, width = x_h.shape
    chunks = tokens // CHUNK
    heads = d_h.shape[0]
    tiles = width // LANES
    frames = o_h.shape[1]
    rows = 16

    small = [
        pltpu.make_async_copy(s, d, in_sem.at[k])
        for k, (s, d) in enumerate(((d_h, d_v), (w_h, w_v), (r_h, r_v), (g_h, g_v), (o_h, o_v)))
    ]

    def columns(t):
        return pl.ds(pl.multiple_of(t * LANES, LANES), LANES)

    def load(t):
        return pltpu.make_async_copy(x_h.at[:, columns(t)], x_v.at[t], x_sem.at[t])

    def load_weight(t):
        return pltpu.make_async_copy(wm_h.at[:, columns(t)], wm_v.at[t], wm_sem.at[t])

    for copy in small + [load(t) for t in range(tiles)]:
        copy.start()

    barrier = pltpu.get_barrier_semaphore()

    def greet(k, _):
        pl.semaphore_signal(
            barrier, inc=1, device_id={"span": lax.rem(me + k, n)}, device_id_type=MESH
        )
        return 0

    lax.fori_loop(1, n, greet, 0)

    row_l, col_l = iota((CHUNK, CHUNK), 0), iota((CHUNK, CHUNK), 1)
    token = token_of_row(row_l)
    lower = ones_where(col_l <= row_l)
    lower_p = ones_where(col_l <= token)
    for k in range(3):
        cum_l[0:CHUNK, k * CHUNK : (k + 1) * CHUNK] = lower
        cum_l[CHUNK : 2 * CHUNK, k * CHUNK : (k + 1) * CHUNK] = lower_p
    head_dim_shift = (width // heads).bit_length() - 1
    expand[...] = ones_where(
        (iota((128, width), 0) & 63) == (iota((128, width), 1) >> head_dim_shift)
    )
    for copy in small:
        copy.wait()

    before = jnp.zeros((1, 128), F32)
    for c in range(chunks):
        part = slice(c * CHUNK, (c + 1) * CHUNK)
        decay = d_v[:, part]
        high = decay.astype(BF16)
        left = decay - high.astype(F32)
        middle = left.astype(BF16)
        low = (left - middle.astype(F32)).astype(BF16)
        parts = jnp.concatenate([high, middle, low], axis=1)
        gap = jnp.zeros((64 - heads, parts.shape[1]), BF16)
        both = dot_t(cum_l[...], jnp.concatenate([parts, gap, parts, gap], axis=0))
        running, running_p = both[0:CHUNK], both[CHUNK : 2 * CHUNK]
        ref = running[CHUNK // 2 - 1 : CHUNK // 2]
        total = running[CHUNK - 1 : CHUNK]
        out_arg[c, 0:CHUNK] = running_p - ref
        out_arg[c, CHUNK : 2 * CHUNK] = running_p + before
        row = iota((16, 128), 0)
        extra = jnp.where(row == 0, ref, jnp.where(row == 1, total, total - ref))
        in_factor[c] = two_parts(jnp.exp(jnp.concatenate([ref - running, extra], axis=0)))
        before = before + total
    owners = o_v[...].astype(F32)
    own_row = jnp.concatenate(
        [jnp.zeros((1, 64), F32), owners, jnp.full((1, 64 - frames), -1.0, F32)], axis=1
    )
    meta_s[...] = jnp.where(iota((1, 128), 1) < 64, before, own_row)

    def summarize(t, _):
        load(t).wait()
        spread = expand[:, columns(t)]
        carry = jnp.zeros((w_v.shape[0], LANES), F32)
        full, scaled = {}, {}
        for k in range(chunks + 2):
            if k < chunks:
                full[k] = dot(in_factor[k], spread)
            c = k - 1
            if 0 <= c < chunks:
                part = slice(c * CHUNK, (c + 1) * CHUNK)
                scaled[c] = (x_v[t, part].astype(F32) * full[c][0:CHUNK]).astype(BF16)
                xs_v[c, t, 0:CHUNK] = scaled[c]
            c = k - 2
            if c >= 0:
                own = dot(w_v[:, c * CHUNK : (c + 1) * CHUNK], scaled.pop(c))
                scales = full.pop(c)[CHUNK : CHUNK + 3]
                xs_v[c, t, CHUNK : CHUNK + 64] = (carry * scales[0:1]).astype(BF16)
                carry = carry * scales[1:2] + own * scales[2:3]
        state[:, columns(t)] = carry
        return 0

    def remote(source, target, sems, d):
        return pltpu.make_async_remote_copy(
            src_ref=source,
            dst_ref=target,
            send_sem=sems.at[0],
            recv_sem=sems.at[1],
            device_id={"span": d},
            device_id_type=MESH,
        )

    def all_of(ref, sem):
        part = ref.at[pl.ds(0, n - 1)]
        pltpu.make_async_copy(part, part, sem).wait()

    def send_meta(k, _):
        remote(meta_s, meta_r.at[me], meta_sem, lax.rem(me + k, n)).start()
        return 0

    def send_half(half):
        for p in range(half, n, 2):
            rows8, cols384 = slice_of(p)
            send1[p] = state[rows8, cols384].astype(BF16)

        def send_one(k, _):
            d = 2 * lax.rem(me // 2 + k, n // 2) + half

            @pl.when(d != me)
            def _():
                remote(send1.at[d], recv1.at[me], one_sem, d).start()

            return 0

        lax.fori_loop(0, n // 2, send_one, 0)

    lax.fori_loop(0, tiles // 2, summarize, 0)
    pl.semaphore_wait(barrier, n - 1)
    lax.fori_loop(1, n, send_meta, 0)
    send_half(0)
    lax.fori_loop(tiles // 2, tiles, summarize, 0)
    send_half(1)
    for t in range(tiles):
        load_weight(t).start()
    meta_r[me] = meta_s[...]
    recv1[me] = send1[me]

    token = token_of_row(iota((CHUNK, CHUNK), 0))
    causal = iota((CHUNK, CHUNK), 1) <= token
    permute = ones_where(iota((CHUNK, CHUNK), 1) == token)

    for c in range(chunks):
        part = slice(c * CHUNK, (c + 1) * CHUNK)
        reads = dot_t(permute, r_v[:, part]).astype(BF16)
        scores = dot(reads, w_v[:, part])
        rp_v[part] = reads
        left_v[c] = jnp.concatenate([jnp.where(causal, scores, 0.0).astype(BF16), reads], axis=1)
        out_factor[c] = two_parts(jnp.exp(out_arg[c]))

    def local(t, _):
        spread = expand[:, columns(t)]
        for c in range(chunks):
            part = slice(c * CHUNK, (c + 1) * CHUNK)
            full = dot(out_factor[c], spread)
            ml_v[t, part] = dot(left_v[c], xs_v[c, t]) * full[0:CHUNK]
            od_v[t, part] = full[CHUNK : 2 * CHUNK]
        return 0

    lax.fori_loop(0, tiles // 2, local, 0)

    all_of(meta_r, meta_sem.at[1])
    meta = meta_r[:, 0, :]
    totals = meta[:, 0:64]
    factors = two_parts(jnp.exp(jnp.concatenate([totals, totals], axis=1)))
    for b in range(4):
        decays[b] = dot(factors, expand[:, 384 * b : 384 * b + 384])
    all_of(recv1, one_sem.at[1])
    quarter = lax.rem(me, 2) * 2 + lax.rem(me // 2, 2)
    carry = jnp.zeros(recv1.shape[1:], F32)
    for i in range(n):
        send2[i] = carry.astype(BF16)
        if i < n - 1:
            carry = carry * decays[quarter, i : i + 1, :] + recv1[i].astype(F32)

    def send_two(k, _):
        d = lax.rem(me + k, n)
        remote(send2.at[d], recv2.at[me], two_sem, d).start()
        return 0

    lax.fori_loop(1, n, send_two, 0)
    recv2[me] = send2[me]
    lax.fori_loop(tiles // 2, tiles, local, 0)
    block_diag[...] = jnp.where(
        (iota((LANES, LANES), 0) >> 6) == (iota((LANES, LANES), 1) >> 6), 1.0 / GROUP, 0.0
    ).astype(BF16)
    owner_rows = jnp.broadcast_to(owners, (8, frames)).astype(BF16)
    spread = ones_where(
        iota((frames, frames * rows), 0) == (iota((frames, frames * rows), 1) >> 4)
    )
    owner_row = dot(owner_rows, spread)[0:1]
    shape = (n * rows, frames * rows)
    sel_s[...] = ones_where(
        ((iota(shape, 0) >> 4).astype(F32) == owner_row)
        & ((iota(shape, 0) & 15) == (iota(shape, 1) & 15))
    )
    mine = (meta == me.astype(F32)) & (iota(meta.shape, 1) >= 64)
    owned = jnp.max(jnp.where(mine, 1.0, 0.0), axis=1, keepdims=True)
    owned = jnp.broadcast_to(owned, (n, 128))
    rank = dot(ones_where(iota((n, n), 1) < iota((n, n), 0)), owned.astype(BF16))
    place = jnp.where(owned > 0.0, rank + 1.0, 0.0)[:, 0:1]
    shape = (n, n * rows)
    place_row = jnp.sum(
        jnp.where((iota(shape, 1) >> 4) == iota(shape, 0), place, 0.0), axis=0, keepdims=True
    )
    shape = (n * rows, n * rows)
    sel_r[...] = ones_where(
        (((iota(shape, 0) >> 4) + 1).astype(F32) == place_row)
        & ((iota(shape, 0) & 15) == (iota(shape, 1) & 15))
    )

    all_of(recv2, two_sem.at[1])
    for p in range(n):
        rows8, cols384 = slice_of(p)
        enter[rows8, cols384] = recv2[p].astype(F32)

    def norm(t, _):
        entering = enter[:, columns(t)].astype(BF16)
        gain = jnp.concatenate([g_v[pl.ds(2 * t, 1), :], g_v[pl.ds(2 * t + 1, 1), :]], axis=1)
        mixed, squares = {}, {}
        for k in range(chunks + 2):
            if k < chunks:
                part = slice(k * CHUNK, (k + 1) * CHUNK)
                mixed[k] = ml_v[t, part] + od_v[t, part] * dot(rp_v[part], entering)
            c = k - 1
            if 0 <= c < chunks:
                squares[c] = dot((mixed[c] * mixed[c]).astype(BF16), block_diag[...])
            c = k - 2
            if c >= 0:
                normed = mixed.pop(c) * lax.rsqrt(squares.pop(c) + EPSILON) * gain
                normed = normed.astype(BF16)
                for q in range(4):
                    first = pl.multiple_of(q * width + t * LANES, LANES)
                    a_v[c * 32 : (c + 1) * 32, pl.ds(first, LANES)] = normed[q * 32 : (q + 1) * 32]
        return 0

    lax.fori_loop(0, tiles, norm, 0)

    z, y, core = me // 8, lax.rem(me // 2, 4), lax.rem(me, 2)
    order = sorted(
        ((dz, dy, dc) for dz in range(4) for dy in range(4) for dc in range(2) if dz + dy + dc),
        key=lambda o: -min(o[0], 4 - o[0]) - min(o[1], 4 - o[1]),
    )

    def place_of(dz, dy, dc):
        return lax.rem(z + dz, 4) * 8 + lax.rem(y + dy, 4) * 2 + lax.rem(core + dc, 2)

    def deliver(t, _):
        load_weight(t).wait()
        merged = dot(a_v[...], wm_v[t]).astype(BF16)
        send3[t] = dot(sel_s[...], merged).astype(BF16).reshape(n, rows, LANES)

        for dz, dy, dc in order:
            d = place_of(dz, dy, dc)
            pltpu.make_async_remote_copy(
                src_ref=send3.at[t, d],
                dst_ref=recv3.at[t, me],
                send_sem=del_s_sem,
                recv_sem=del_r_sem.at[t],
                device_id={"span": d},
                device_id_type=MESH,
            ).start()
        recv3[t, me] = send3[t, me]
        return 0

    lax.fori_loop(0, tiles, deliver, 0)

    def arrive(t, _):
        part = recv3.at[t, pl.ds(0, n - 1)]
        pltpu.make_async_copy(part, part, del_r_sem.at[t]).wait()
        out_h[:, columns(t)] = dot(
            sel_r[...], recv3[t].reshape(n * rows, LANES)
        ).astype(BF16)
        return 0

    lax.fori_loop(0, tiles, arrive, 0)
    one_meta = meta_r.at[pl.ds(0, n - 1)]
    pltpu.make_async_copy(one_meta, one_meta, meta_sem.at[0]).wait()
    all_of(send1, one_sem.at[0])
    all_of(send2, two_sem.at[0])

    def sent(t, _):
        part = send3.at[t, pl.ds(0, n - 1)]
        pltpu.make_async_copy(part, part, del_s_sem).wait()
        return 0

    lax.fori_loop(0, tiles, sent, 0)


def shards(heads_in, writer, reader, log_decay, norm_gain, merge_weight, frame_owner):
    tokens, width = heads_in.shape
    n = lax.axis_size("span")
    chunks = tokens // CHUNK
    tiles = width // LANES
    frames = frame_owner.shape[0]
    state_size = writer.shape[1]
    deep, out_width = merge_weight.shape
    assert (n, state_size, width, out_width, frames) == (32, 64, 1536, 1536, 16)
    vmem, dma = pltpu.VMEM, pltpu.SemaphoreType.DMA
    in_place = pl.BlockSpec(memory_space=pltpu.HBM)
    return pl.pallas_call(
        functools.partial(kernel, n),
        out_shape=pltpu.VMEM((n * 16, out_width), BF16),
        in_specs=[in_place] * 7,
        out_specs=pl.BlockSpec(memory_space=pltpu.VMEM),
        scratch_shapes=[
            vmem((tiles, tokens, LANES), BF16),
            vmem(writer.shape[::-1], BF16),
            vmem(reader.shape[::-1], BF16),
            vmem(log_decay.shape[::-1], F32),
            vmem((width // 128, 128), F32),
            vmem((1, frames), jnp.int32),
            vmem((tiles, deep, LANES), BF16),
            vmem((2 * CHUNK, 3 * CHUNK), BF16),
            vmem((128, width), BF16),
            vmem((LANES, LANES), BF16),
            vmem((chunks, tiles, CHUNK + state_size, LANES), BF16),
            vmem((chunks, CHUNK + 16, 128), BF16),
            vmem((chunks, 2 * CHUNK, 128), F32),
            vmem((chunks, 2 * CHUNK, 128), BF16),
            vmem((chunks, CHUNK, CHUNK + state_size), BF16),
            vmem((state_size, width), F32),
            vmem((tokens, state_size), BF16),
            vmem((tiles, tokens, LANES), F32),
            vmem((tiles, tokens, LANES), F32),
            vmem((tokens // 4, deep), BF16),
            vmem((1, 128), F32),
            vmem((n, 1, 128), F32),
            vmem((n, 8, 384), BF16),
            vmem((n, 8, 384), BF16),
            vmem((4, n, 384), F32),
            vmem((n, 8, 384), BF16),
            vmem((n, 8, 384), BF16),
            vmem((state_size, width), F32),
            vmem((n * 16, frames * 16), BF16),
            vmem((n * 16, n * 16), BF16),
            vmem((tiles, n, 16, LANES), BF16),
            vmem((tiles, n, 16, LANES), BF16),
            dma((tiles,)),
            dma((5,)),
            dma((tiles,)),
            dma((2,)),
            dma((2,)),
            dma((2,)),
            dma,
            dma((tiles,)),
        ],
        compiler_params=pltpu.CompilerParams(
            collective_id=0, has_side_effects=True, vmem_limit_bytes=52 * 1024 * 1024
        ),
    )(
        *(
            pltpu.with_memory_space_constraint(array, pltpu.HBM)
            for array in (
                heads_in,
                writer.T,
                reader.T,
                log_decay.T,
                norm_gain.reshape(width // 128, 128),
                frame_owner.reshape(1, frames),
                merge_weight,
            )
        )
    )


def solution(mesh):
    return jax.shard_map(
        shards,
        mesh=mesh,
        in_specs=(
            P(("batch", "span"), None),
            P(("batch", "span"), None),
            P(("batch", "span"), None),
            P(("batch", "span"), None),
            P(),
            P(),
            P(("batch", "span")),
        ),
        out_specs=P(("batch", "span"), None),
        check_vma=False,
    )
```

```python
import functools

import jax
import jax.numpy as jnp
from jax import lax
from jax.experimental import pallas as pl
from jax.experimental.pallas import tpu as pltpu
from jax.sharding import PartitionSpec as P

MESH = pl.DeviceIdType.MESH
F32 = jnp.float32
BF16 = jnp.bfloat16
EPSILON = 1e-05
FRAME_SIDE = 8
CHUNK = 128
LANES = 256
GROUP = 64


def dot(a, b):
    return lax.dot_general(a, b, (((1,), (0,)), ((), ())), preferred_element_type=F32)


def dot_t(a, b):
    return lax.dot_general(a, b, (((1,), (1,)), ((), ())), preferred_element_type=F32)


def iota(shape, axis):
    return lax.broadcasted_iota(jnp.int32, shape, axis)


def ones_where(condition):
    return jnp.where(condition, 1.0, 0.0).astype(BF16)


def slice_of(p):
    b = (p & 1) * 2 + ((p >> 1) & 1)
    return slice(8 * (p >> 2), 8 * (p >> 2) + 8), slice(384 * b, 384 * b + 384)


def token_of_row(row):
    q, rest = row >> 5, row & 31
    frame, i2, j2 = rest >> 4, (rest >> 2) & 3, rest & 3
    return frame * 64 + (2 * i2 + (q >> 1)) * 8 + 2 * j2 + (q & 1)


def two_parts(values):
    high = values.astype(BF16)
    low = (values - high.astype(F32)).astype(BF16)
    return jnp.where(iota(values.shape, 1) < 64, high.astype(F32), low.astype(F32)).astype(BF16)


def kernel(
    n, x_h, w_h, r_h, d_h, g_h, o_h, wm_h, out_h,
    x_v, w_v, r_v, d_v, g_v, o_v, wm_v,
    cum_l, expand, block_diag, xs_v, in_factor, out_arg, out_factor, left_v, state, rp_v, ml_v, od_v, a_v,
    meta_s, meta_r, send1, recv1, decays, send2, recv2, enter, sel_s, sel_r, send3, recv3,
    x_sem, in_sem, wm_sem, meta_sem, one_sem, two_sem, del_s_sem, del_r_sem,
):
    me = lax.axis_index("span")
    tokens, width = x_h.shape
    chunks = tokens // CHUNK
    heads = d_h.shape[0]
    tiles = width // LANES
    frames = o_h.shape[1]
    rows = 16

    small = [
        pltpu.make_async_copy(s, d, in_sem.at[k])
        for k, (s, d) in enumerate(((d_h, d_v), (w_h, w_v), (r_h, r_v), (g_h, g_v), (o_h, o_v)))
    ]

    def columns(t):
        return pl.ds(pl.multiple_of(t * LANES, LANES), LANES)

    def load(t):
        return pltpu.make_async_copy(x_h.at[:, columns(t)], x_v.at[t], x_sem.at[t])

    def load_weight(t):
        return pltpu.make_async_copy(wm_h.at[:, columns(t)], wm_v.at[t], wm_sem.at[t])

    for copy in small + [load(t) for t in range(tiles)]:
        copy.start()

    barrier = pltpu.get_barrier_semaphore()

    def greet(k, _):
        pl.semaphore_signal(
            barrier, inc=1, device_id={"span": lax.rem(me + k, n)}, device_id_type=MESH
        )
        return 0

    lax.fori_loop(1, n, greet, 0)

    row_l, col_l = iota((CHUNK, CHUNK), 0), iota((CHUNK, CHUNK), 1)
    token = token_of_row(row_l)
    lower = ones_where(col_l <= row_l)
    lower_p = ones_where(col_l <= token)
    for k in range(3):
        cum_l[0:CHUNK, k * CHUNK : (k + 1) * CHUNK] = lower
        cum_l[CHUNK : 2 * CHUNK, k * CHUNK : (k + 1) * CHUNK] = lower_p
    head_dim_shift = (width // heads).bit_length() - 1
    expand[...] = ones_where(
        (iota((128, width), 0) & 63) == (iota((128, width), 1) >> head_dim_shift)
    )
    for copy in small:
        copy.wait()

    before = jnp.zeros((1, 128), F32)
    for c in range(chunks):
        part = slice(c * CHUNK, (c + 1) * CHUNK)
        decay = d_v[:, part]
        high = decay.astype(BF16)
        left = decay - high.astype(F32)
        middle = left.astype(BF16)
        low = (left - middle.astype(F32)).astype(BF16)
        parts = jnp.concatenate([high, middle, low], axis=1)
        gap = jnp.zeros((64 - heads, parts.shape[1]), BF16)
        both = dot_t(cum_l[...], jnp.concatenate([parts, gap, parts, gap], axis=0))
        running, running_p = both[0:CHUNK], both[CHUNK : 2 * CHUNK]
        ref = running[CHUNK // 2 - 1 : CHUNK // 2]
        total = running[CHUNK - 1 : CHUNK]
        out_arg[c, 0:CHUNK] = running_p - ref
        out_arg[c, CHUNK : 2 * CHUNK] = running_p + before
        row = iota((16, 128), 0)
        extra = jnp.where(row == 0, ref, jnp.where(row == 1, total, total - ref))
        in_factor[c] = two_parts(jnp.exp(jnp.concatenate([ref - running, extra], axis=0)))
        before = before + total
    owners = o_v[...].astype(F32)
    own_row = jnp.concatenate(
        [jnp.zeros((1, 64), F32), owners, jnp.full((1, 64 - frames), -1.0, F32)], axis=1
    )
    meta_s[...] = jnp.where(iota((1, 128), 1) < 64, before, own_row)

    def summarize(t, _):
        load(t).wait()
        spread = expand[:, columns(t)]
        carry = jnp.zeros((w_v.shape[0], LANES), F32)
        full, scaled = {}, {}
        for k in range(chunks + 2):
            if k < chunks:
                full[k] = dot(in_factor[k], spread)
            c = k - 1
            if 0 <= c < chunks:
                part = slice(c * CHUNK, (c + 1) * CHUNK)
                scaled[c] = (x_v[t, part].astype(F32) * full[c][0:CHUNK]).astype(BF16)
                xs_v[c, t, 0:CHUNK] = scaled[c]
            c = k - 2
            if c >= 0:
                own = dot(w_v[:, c * CHUNK : (c + 1) * CHUNK], scaled.pop(c))
                scales = full.pop(c)[CHUNK : CHUNK + 3]
                xs_v[c, t, CHUNK : CHUNK + 64] = (carry * scales[0:1]).astype(BF16)
                carry = carry * scales[1:2] + own * scales[2:3]
        state[:, columns(t)] = carry
        return 0

    def remote(source, target, sems, d):
        return pltpu.make_async_remote_copy(
            src_ref=source,
            dst_ref=target,
            send_sem=sems.at[0],
            recv_sem=sems.at[1],
            device_id={"span": d},
            device_id_type=MESH,
        )

    def all_of(ref, sem):
        part = ref.at[pl.ds(0, n - 1)]
        pltpu.make_async_copy(part, part, sem).wait()

    z, y, core = me // 8, lax.rem(me // 2, 4), lax.rem(me, 2)
    order = sorted(
        ((dz, dy, dc) for dz in range(4) for dy in range(4) for dc in range(2) if dz + dy + dc),
        key=lambda o: -min(o[0], 4 - o[0]) - min(o[1], 4 - o[1]),
    )

    def place_of(dz, dy, dc):
        return lax.rem(z + dz, 4) * 8 + lax.rem(y + dy, 4) * 2 + lax.rem(core + dc, 2)

    def send_meta(k, _):
        remote(meta_s, meta_r.at[me], meta_sem, lax.rem(me + k, n)).start()
        return 0

    def send_half(half):
        for p in range(half, n, 2):
            rows8, cols384 = slice_of(p)
            send1[p] = state[rows8, cols384].astype(BF16)

        for dz, dy, dc in order + [(0, 0, 0)]:
            if dc == 0:
                d = lax.rem(z + dz, 4) * 8 + lax.rem(y + dy, 4) * 2 + half

                @pl.when(d != me)
                def _():
                    remote(send1.at[d], recv1.at[me], one_sem, d).start()

    lax.fori_loop(0, tiles // 2, summarize, 0)
    pl.semaphore_wait(barrier, n - 1)
    lax.fori_loop(1, n, send_meta, 0)
    send_half(0)
    lax.fori_loop(tiles // 2, tiles, summarize, 0)
    send_half(1)
    for t in range(tiles):
        load_weight(t).start()
    meta_r[me] = meta_s[...]
    recv1[me] = send1[me]

    token = token_of_row(iota((CHUNK, CHUNK), 0))
    causal = iota((CHUNK, CHUNK), 1) <= token
    permute = ones_where(iota((CHUNK, CHUNK), 1) == token)

    for c in range(chunks):
        part = slice(c * CHUNK, (c + 1) * CHUNK)
        reads = dot_t(permute, r_v[:, part]).astype(BF16)
        scores = dot(reads, w_v[:, part])
        rp_v[part] = reads
        left_v[c] = jnp.concatenate([jnp.where(causal, scores, 0.0).astype(BF16), reads], axis=1)
        out_factor[c] = two_parts(jnp.exp(out_arg[c]))

    def local(t, _):
        spread = expand[:, columns(t)]
        for c in range(chunks):
            part = slice(c * CHUNK, (c + 1) * CHUNK)
            full = dot(out_factor[c], spread)
            ml_v[t, part] = dot(left_v[c], xs_v[c, t]) * full[0:CHUNK]
            od_v[t, part] = full[CHUNK : 2 * CHUNK]
        return 0

    lax.fori_loop(0, tiles // 2, local, 0)

    all_of(meta_r, meta_sem.at[1])
    meta = meta_r[:, 0, :]
    totals = meta[:, 0:64]
    factors = two_parts(jnp.exp(jnp.concatenate([totals, totals], axis=1)))
    for b in range(4):
        decays[b] = dot(factors, expand[:, 384 * b : 384 * b + 384])
    all_of(recv1, one_sem.at[1])
    quarter = lax.rem(me, 2) * 2 + lax.rem(me // 2, 2)
    carry = jnp.zeros(recv1.shape[1:], F32)
    for i in range(n):
        send2[i] = carry.astype(BF16)
        if i < n - 1:
            carry = carry * decays[quarter, i : i + 1, :] + recv1[i].astype(F32)

    for dz, dy, dc in order:
        d = place_of(dz, dy, dc)
        remote(send2.at[d], recv2.at[me], two_sem, d).start()
    recv2[me] = send2[me]
    lax.fori_loop(tiles // 2, tiles, local, 0)
    block_diag[...] = jnp.where(
        (iota((LANES, LANES), 0) >> 6) == (iota((LANES, LANES), 1) >> 6), 1.0 / GROUP, 0.0
    ).astype(BF16)
    owner_rows = jnp.broadcast_to(owners, (8, frames)).astype(BF16)
    spread = ones_where(
        iota((frames, frames * rows), 0) == (iota((frames, frames * rows), 1) >> 4)
    )
    owner_row = dot(owner_rows, spread)[0:1]
    shape = (n * rows, frames * rows)
    sel_s[...] = ones_where(
        ((iota(shape, 0) >> 4).astype(F32) == owner_row)
        & ((iota(shape, 0) & 15) == (iota(shape, 1) & 15))
    )
    mine = (meta == me.astype(F32)) & (iota(meta.shape, 1) >= 64)
    owned = jnp.max(jnp.where(mine, 1.0, 0.0), axis=1, keepdims=True)
    owned = jnp.broadcast_to(owned, (n, 128))
    rank = dot(ones_where(iota((n, n), 1) < iota((n, n), 0)), owned.astype(BF16))
    place = jnp.where(owned > 0.0, rank + 1.0, 0.0)[:, 0:1]
    shape = (n, n * rows)
    place_row = jnp.sum(
        jnp.where((iota(shape, 1) >> 4) == iota(shape, 0), place, 0.0), axis=0, keepdims=True
    )
    shape = (n * rows, n * rows)
    sel_r[...] = ones_where(
        (((iota(shape, 0) >> 4) + 1).astype(F32) == place_row)
        & ((iota(shape, 0) & 15) == (iota(shape, 1) & 15))
    )

    all_of(recv2, two_sem.at[1])
    for p in range(n):
        rows8, cols384 = slice_of(p)
        enter[rows8, cols384] = recv2[p].astype(F32)

    def norm(t, _):
        entering = enter[:, columns(t)].astype(BF16)
        gain = jnp.concatenate([g_v[pl.ds(2 * t, 1), :], g_v[pl.ds(2 * t + 1, 1), :]], axis=1)
        mixed, squares = {}, {}
        for k in range(chunks + 2):
            if k < chunks:
                part = slice(k * CHUNK, (k + 1) * CHUNK)
                mixed[k] = ml_v[t, part] + od_v[t, part] * dot(rp_v[part], entering)
            c = k - 1
            if 0 <= c < chunks:
                squares[c] = dot((mixed[c] * mixed[c]).astype(BF16), block_diag[...])
            c = k - 2
            if c >= 0:
                normed = mixed.pop(c) * lax.rsqrt(squares.pop(c) + EPSILON) * gain
                normed = normed.astype(BF16)
                for q in range(4):
                    first = pl.multiple_of(q * width + t * LANES, LANES)
                    a_v[c * 32 : (c + 1) * 32, pl.ds(first, LANES)] = normed[q * 32 : (q + 1) * 32]
        return 0

    lax.fori_loop(0, tiles, norm, 0)

    def deliver(t, _):
        load_weight(t).wait()
        merged = dot(a_v[...], wm_v[t]).astype(BF16)
        send3[t] = dot(sel_s[...], merged).astype(BF16).reshape(n, rows, LANES)

        for dz, dy, dc in order:
            d = place_of(dz, dy, dc)
            pltpu.make_async_remote_copy(
                src_ref=send3.at[t, d],
                dst_ref=recv3.at[t, me],
                send_sem=del_s_sem,
                recv_sem=del_r_sem.at[t],
                device_id={"span": d},
                device_id_type=MESH,
            ).start()
        recv3[t, me] = send3[t, me]
        return 0

    lax.fori_loop(0, tiles, deliver, 0)

    def arrive(t, _):
        part = recv3.at[t, pl.ds(0, n - 1)]
        pltpu.make_async_copy(part, part, del_r_sem.at[t]).wait()
        out_h[:, columns(t)] = dot(
            sel_r[...], recv3[t].reshape(n * rows, LANES)
        ).astype(BF16)
        return 0

    lax.fori_loop(0, tiles, arrive, 0)
    one_meta = meta_r.at[pl.ds(0, n - 1)]
    pltpu.make_async_copy(one_meta, one_meta, meta_sem.at[0]).wait()
    all_of(send1, one_sem.at[0])
    all_of(send2, two_sem.at[0])

    def sent(t, _):
        part = send3.at[t, pl.ds(0, n - 1)]
        pltpu.make_async_copy(part, part, del_s_sem).wait()
        return 0

    lax.fori_loop(0, tiles, sent, 0)


def shards(heads_in, writer, reader, log_decay, norm_gain, merge_weight, frame_owner):
    tokens, width = heads_in.shape
    n = lax.axis_size("span")
    chunks = tokens // CHUNK
    tiles = width // LANES
    frames = frame_owner.shape[0]
    state_size = writer.shape[1]
    deep, out_width = merge_weight.shape
    assert (n, state_size, width, out_width, frames) == (32, 64, 1536, 1536, 16)
    vmem, dma = pltpu.VMEM, pltpu.SemaphoreType.DMA
    in_place = pl.BlockSpec(memory_space=pltpu.HBM)
    return pl.pallas_call(
        functools.partial(kernel, n),
        out_shape=pltpu.VMEM((n * 16, out_width), BF16),
        in_specs=[in_place] * 7,
        out_specs=pl.BlockSpec(memory_space=pltpu.VMEM),
        scratch_shapes=[
            vmem((tiles, tokens, LANES), BF16),
            vmem(writer.shape[::-1], BF16),
            vmem(reader.shape[::-1], BF16),
            vmem(log_decay.shape[::-1], F32),
            vmem((width // 128, 128), F32),
            vmem((1, frames), jnp.int32),
            vmem((tiles, deep, LANES), BF16),
            vmem((2 * CHUNK, 3 * CHUNK), BF16),
            vmem((128, width), BF16),
            vmem((LANES, LANES), BF16),
            vmem((chunks, tiles, CHUNK + state_size, LANES), BF16),
            vmem((chunks, CHUNK + 16, 128), BF16),
            vmem((chunks, 2 * CHUNK, 128), F32),
            vmem((chunks, 2 * CHUNK, 128), BF16),
            vmem((chunks, CHUNK, CHUNK + state_size), BF16),
            vmem((state_size, width), F32),
            vmem((tokens, state_size), BF16),
            vmem((tiles, tokens, LANES), F32),
            vmem((tiles, tokens, LANES), F32),
            vmem((tokens // 4, deep), BF16),
            vmem((1, 128), F32),
            vmem((n, 1, 128), F32),
            vmem((n, 8, 384), BF16),
            vmem((n, 8, 384), BF16),
            vmem((4, n, 384), F32),
            vmem((n, 8, 384), BF16),
            vmem((n, 8, 384), BF16),
            vmem((state_size, width), F32),
            vmem((n * 16, frames * 16), BF16),
            vmem((n * 16, n * 16), BF16),
            vmem((tiles, n, 16, LANES), BF16),
            vmem((tiles, n, 16, LANES), BF16),
            dma((tiles,)),
            dma((5,)),
            dma((tiles,)),
            dma((2,)),
            dma((2,)),
            dma((2,)),
            dma,
            dma((tiles,)),
        ],
        compiler_params=pltpu.CompilerParams(
            collective_id=0, has_side_effects=True, vmem_limit_bytes=52 * 1024 * 1024
        ),
    )(
        *(
            pltpu.with_memory_space_constraint(array, pltpu.HBM)
            for array in (
                heads_in,
                writer.T,
                reader.T,
                log_decay.T,
                norm_gain.reshape(width // 128, 128),
                frame_owner.reshape(1, frames),
                merge_weight,
            )
        )
    )


def solution(mesh):
    return jax.shard_map(
        shards,
        mesh=mesh,
        in_specs=(
            P(("batch", "span"), None),
            P(("batch", "span"), None),
            P(("batch", "span"), None),
            P(("batch", "span"), None),
            P(),
            P(),
            P(("batch", "span")),
        ),
        out_specs=P(("batch", "span"), None),
        check_vma=False,
    )
```

```python
import functools

import jax
import jax.numpy as jnp
from jax import lax
from jax.experimental import pallas as pl
from jax.experimental.pallas import tpu as pltpu
from jax.sharding import PartitionSpec as P

MESH = pl.DeviceIdType.MESH
F32 = jnp.float32
BF16 = jnp.bfloat16
EPSILON = 1e-05
FRAME_SIDE = 8
CHUNK = 128
LANES = 256
GROUP = 64


def dot(a, b):
    return lax.dot_general(a, b, (((1,), (0,)), ((), ())), preferred_element_type=F32)


def dot_t(a, b):
    return lax.dot_general(a, b, (((1,), (1,)), ((), ())), preferred_element_type=F32)


def iota(shape, axis):
    return lax.broadcasted_iota(jnp.int32, shape, axis)


def ones_where(condition):
    return jnp.where(condition, 1.0, 0.0).astype(BF16)


def slice_of(p):
    b = (p & 1) * 2 + ((p >> 1) & 1)
    return slice(8 * (p >> 2), 8 * (p >> 2) + 8), slice(384 * b, 384 * b + 384)


def token_of_row(row):
    q, rest = row >> 5, row & 31
    frame, i2, j2 = rest >> 4, (rest >> 2) & 3, rest & 3
    return frame * 64 + (2 * i2 + (q >> 1)) * 8 + 2 * j2 + (q & 1)


def widen(factor, tile):
    lane = tile * 8 + (iota(factor.shape, 1) >> 5)
    pick = functools.partial(jnp.take_along_axis, factor, axis=1, mode="promise_in_bounds")
    return jnp.concatenate([pick(lane), pick(lane + 4)], axis=1)


def two_parts(values):
    high = values.astype(BF16)
    low = (values - high.astype(F32)).astype(BF16)
    return jnp.where(iota(values.shape, 1) < 64, high.astype(F32), low.astype(F32)).astype(BF16)


def kernel(
    n, x_h, w_h, r_h, d_h, g_h, o_h, wm_h, out_h,
    x_v, w_v, r_v, d_v, g_v, o_v, wm_v,
    cum_l, expand, block_diag, xs_v, in_factor, out_arg, out_factor, left_v, state, rp_v, ml_v, od_v, a_v,
    meta_s, meta_r, send1, recv1, decays, send2, recv2, enter, sel_s, sel_r, send3, recv3,
    x_sem, in_sem, wm_sem, meta_sem, one_sem, two_sem, del_s_sem, del_r_sem,
):
    me = lax.axis_index("span")
    tokens, width = x_h.shape
    chunks = tokens // CHUNK
    heads = d_h.shape[0]
    tiles = width // LANES
    frames = o_h.shape[1]
    rows = 16

    small = [
        pltpu.make_async_copy(s, d, in_sem.at[k])
        for k, (s, d) in enumerate(((d_h, d_v), (w_h, w_v), (r_h, r_v), (g_h, g_v), (o_h, o_v)))
    ]

    def columns(t):
        return pl.ds(pl.multiple_of(t * LANES, LANES), LANES)

    def load(t):
        return pltpu.make_async_copy(x_h.at[:, columns(t)], x_v.at[t], x_sem.at[t])

    def load_weight(t):
        return pltpu.make_async_copy(wm_h.at[:, columns(t)], wm_v.at[t], wm_sem.at[t])

    for copy in small + [load(t) for t in range(tiles)]:
        copy.start()

    barrier = pltpu.get_barrier_semaphore()

    def greet(k, _):
        pl.semaphore_signal(
            barrier, inc=1, device_id={"span": lax.rem(me + k, n)}, device_id_type=MESH
        )
        return 0

    lax.fori_loop(1, n, greet, 0)

    row_l, col_l = iota((CHUNK, CHUNK), 0), iota((CHUNK, CHUNK), 1)
    token = token_of_row(row_l)
    lower = ones_where(col_l <= row_l)
    lower_p = ones_where(col_l <= token)
    for k in range(3):
        cum_l[0:CHUNK, k * CHUNK : (k + 1) * CHUNK] = lower
        cum_l[CHUNK : 2 * CHUNK, k * CHUNK : (k + 1) * CHUNK] = lower_p
    head_dim_shift = (width // heads).bit_length() - 1
    expand[...] = ones_where(
        (iota((128, width), 0) & 63) == (iota((128, width), 1) >> head_dim_shift)
    )
    for copy in small:
        copy.wait()

    before = jnp.zeros((1, 128), F32)
    for c in range(chunks):
        part = slice(c * CHUNK, (c + 1) * CHUNK)
        decay = d_v[:, part]
        high = decay.astype(BF16)
        left = decay - high.astype(F32)
        middle = left.astype(BF16)
        low = (left - middle.astype(F32)).astype(BF16)
        parts = jnp.concatenate([high, middle, low], axis=1)
        gap = jnp.zeros((64 - heads, parts.shape[1]), BF16)
        both = dot_t(cum_l[...], jnp.concatenate([parts, gap, parts, gap], axis=0))
        running, running_p = both[0:CHUNK], both[CHUNK : 2 * CHUNK]
        ref = running[CHUNK // 2 - 1 : CHUNK // 2]
        total = running[CHUNK - 1 : CHUNK]
        out_arg[c, 0:CHUNK] = running_p - ref
        out_arg[c, CHUNK : 2 * CHUNK] = running_p + before
        row = iota((16, 128), 0)
        extra = jnp.where(row == 0, ref, jnp.where(row == 1, total, total - ref))
        in_factor[c] = jnp.exp(jnp.concatenate([ref - running, extra], axis=0))
        before = before + total
    owners = o_v[...].astype(F32)
    own_row = jnp.concatenate(
        [jnp.zeros((1, 64), F32), owners, jnp.full((1, 64 - frames), -1.0, F32)], axis=1
    )
    meta_s[...] = jnp.where(iota((1, 128), 1) < 64, before, own_row)

    def summarize(t, _):
        load(t).wait()
        carry = jnp.zeros((w_v.shape[0], LANES), F32)
        full, scaled = {}, {}
        for k in range(chunks + 2):
            if k < chunks:
                full[k] = widen(in_factor[k], t)
            c = k - 1
            if 0 <= c < chunks:
                part = slice(c * CHUNK, (c + 1) * CHUNK)
                scaled[c] = (x_v[t, part].astype(F32) * full[c][0:CHUNK]).astype(BF16)
                xs_v[c, t, 0:CHUNK] = scaled[c]
            c = k - 2
            if c >= 0:
                own = dot(w_v[:, c * CHUNK : (c + 1) * CHUNK], scaled.pop(c))
                scales = full.pop(c)[CHUNK : CHUNK + 3]
                xs_v[c, t, CHUNK : CHUNK + 64] = (carry * scales[0:1]).astype(BF16)
                carry = carry * scales[1:2] + own * scales[2:3]
        state[:, columns(t)] = carry
        return 0

    def remote(source, target, sems, d):
        return pltpu.make_async_remote_copy(
            src_ref=source,
            dst_ref=target,
            send_sem=sems.at[0],
            recv_sem=sems.at[1],
            device_id={"span": d},
            device_id_type=MESH,
        )

    def all_of(ref, sem):
        part = ref.at[pl.ds(0, n - 1)]
        pltpu.make_async_copy(part, part, sem).wait()

    z, y, core = me // 8, lax.rem(me // 2, 4), lax.rem(me, 2)
    order = sorted(
        ((dz, dy, dc) for dz in range(4) for dy in range(4) for dc in range(2) if dz + dy + dc),
        key=lambda o: -min(o[0], 4 - o[0]) - min(o[1], 4 - o[1]),
    )

    def place_of(dz, dy, dc):
        return lax.rem(z + dz, 4) * 8 + lax.rem(y + dy, 4) * 2 + lax.rem(core + dc, 2)

    def send_meta(k, _):
        remote(meta_s, meta_r.at[me], meta_sem, lax.rem(me + k, n)).start()
        return 0

    def send_half(half):
        for p in range(half, n, 2):
            rows8, cols384 = slice_of(p)
            send1[p] = state[rows8, cols384].astype(BF16)

        for dz, dy, dc in order + [(0, 0, 0)]:
            if dc == 0:
                d = lax.rem(z + dz, 4) * 8 + lax.rem(y + dy, 4) * 2 + half

                @pl.when(d != me)
                def _():
                    remote(send1.at[d], recv1.at[me], one_sem, d).start()

    lax.fori_loop(0, tiles // 2, summarize, 0)
    pl.semaphore_wait(barrier, n - 1)
    lax.fori_loop(1, n, send_meta, 0)
    send_half(0)
    lax.fori_loop(tiles // 2, tiles, summarize, 0)
    send_half(1)
    for t in range(tiles):
        load_weight(t).start()
    meta_r[me] = meta_s[...]
    recv1[me] = send1[me]

    token = token_of_row(iota((CHUNK, CHUNK), 0))
    causal = iota((CHUNK, CHUNK), 1) <= token
    permute = ones_where(iota((CHUNK, CHUNK), 1) == token)

    for c in range(chunks):
        part = slice(c * CHUNK, (c + 1) * CHUNK)
        reads = dot_t(permute, r_v[:, part]).astype(BF16)
        scores = dot(reads, w_v[:, part])
        rp_v[part] = reads
        left_v[c] = jnp.concatenate([jnp.where(causal, scores, 0.0).astype(BF16), reads], axis=1)
        out_factor[c] = two_parts(jnp.exp(out_arg[c]))

    def local(t, _):
        spread = expand[:, columns(t)]
        for c in range(chunks):
            part = slice(c * CHUNK, (c + 1) * CHUNK)
            full = dot(out_factor[c], spread)
            ml_v[t, part] = dot(left_v[c], xs_v[c, t]) * full[0:CHUNK]
            od_v[t, part] = full[CHUNK : 2 * CHUNK]
        return 0

    lax.fori_loop(0, tiles // 2, local, 0)

    all_of(meta_r, meta_sem.at[1])
    meta = meta_r[:, 0, :]
    totals = meta[:, 0:64]
    factors = two_parts(jnp.exp(jnp.concatenate([totals, totals], axis=1)))
    for b in range(4):
        decays[b] = dot(factors, expand[:, 384 * b : 384 * b + 384])
    all_of(recv1, one_sem.at[1])
    quarter = lax.rem(me, 2) * 2 + lax.rem(me // 2, 2)
    carry = jnp.zeros(recv1.shape[1:], F32)
    for i in range(n):
        send2[i] = carry.astype(BF16)
        if i < n - 1:
            carry = carry * decays[quarter, i : i + 1, :] + recv1[i].astype(F32)

    for dz, dy, dc in order:
        d = place_of(dz, dy, dc)
        remote(send2.at[d], recv2.at[me], two_sem, d).start()
    recv2[me] = send2[me]
    lax.fori_loop(tiles // 2, tiles, local, 0)
    block_diag[...] = jnp.where(
        (iota((LANES, LANES), 0) >> 6) == (iota((LANES, LANES), 1) >> 6), 1.0 / GROUP, 0.0
    ).astype(BF16)
    owner_rows = jnp.broadcast_to(owners, (8, frames)).astype(BF16)
    spread = ones_where(
        iota((frames, frames * rows), 0) == (iota((frames, frames * rows), 1) >> 4)
    )
    owner_row = dot(owner_rows, spread)[0:1]
    shape = (n * rows, frames * rows)
    sel_s[...] = ones_where(
        ((iota(shape, 0) >> 4).astype(F32) == owner_row)
        & ((iota(shape, 0) & 15) == (iota(shape, 1) & 15))
    )
    mine = (meta == me.astype(F32)) & (iota(meta.shape, 1) >= 64)
    owned = jnp.max(jnp.where(mine, 1.0, 0.0), axis=1, keepdims=True)
    owned = jnp.broadcast_to(owned, (n, 128))
    rank = dot(ones_where(iota((n, n), 1) < iota((n, n), 0)), owned.astype(BF16))
    place = jnp.where(owned > 0.0, rank + 1.0, 0.0)[:, 0:1]
    shape = (n, n * rows)
    place_row = jnp.sum(
        jnp.where((iota(shape, 1) >> 4) == iota(shape, 0), place, 0.0), axis=0, keepdims=True
    )
    shape = (n * rows, n * rows)
    sel_r[...] = ones_where(
        (((iota(shape, 0) >> 4) + 1).astype(F32) == place_row)
        & ((iota(shape, 0) & 15) == (iota(shape, 1) & 15))
    )

    all_of(recv2, two_sem.at[1])
    for p in range(n):
        rows8, cols384 = slice_of(p)
        enter[rows8, cols384] = recv2[p].astype(F32)

    def norm(t, _):
        entering = enter[:, columns(t)].astype(BF16)
        gain = jnp.concatenate([g_v[pl.ds(2 * t, 1), :], g_v[pl.ds(2 * t + 1, 1), :]], axis=1)
        mixed, squares = {}, {}
        for k in range(chunks + 2):
            if k < chunks:
                part = slice(k * CHUNK, (k + 1) * CHUNK)
                mixed[k] = ml_v[t, part] + od_v[t, part] * dot(rp_v[part], entering)
            c = k - 1
            if 0 <= c < chunks:
                squares[c] = dot((mixed[c] * mixed[c]).astype(BF16), block_diag[...])
            c = k - 2
            if c >= 0:
                normed = mixed.pop(c) * lax.rsqrt(squares.pop(c) + EPSILON) * gain
                normed = normed.astype(BF16)
                for q in range(4):
                    first = pl.multiple_of(q * width + t * LANES, LANES)
                    a_v[c * 32 : (c + 1) * 32, pl.ds(first, LANES)] = normed[q * 32 : (q + 1) * 32]
        return 0

    lax.fori_loop(0, tiles, norm, 0)

    def deliver(t, _):
        load_weight(t).wait()
        merged = dot(a_v[...], wm_v[t]).astype(BF16)
        send3[t] = dot(sel_s[...], merged).astype(BF16).reshape(n, rows, LANES)

        for dz, dy, dc in order:
            d = place_of(dz, dy, dc)
            pltpu.make_async_remote_copy(
                src_ref=send3.at[t, d],
                dst_ref=recv3.at[t, me],
                send_sem=del_s_sem,
                recv_sem=del_r_sem.at[t],
                device_id={"span": d},
                device_id_type=MESH,
            ).start()
        recv3[t, me] = send3[t, me]
        return 0

    lax.fori_loop(0, tiles, deliver, 0)

    def arrive(t, _):
        part = recv3.at[t, pl.ds(0, n - 1)]
        pltpu.make_async_copy(part, part, del_r_sem.at[t]).wait()
        out_h[:, columns(t)] = dot(
            sel_r[...], recv3[t].reshape(n * rows, LANES)
        ).astype(BF16)
        return 0

    lax.fori_loop(0, tiles, arrive, 0)
    one_meta = meta_r.at[pl.ds(0, n - 1)]
    pltpu.make_async_copy(one_meta, one_meta, meta_sem.at[0]).wait()
    all_of(send1, one_sem.at[0])
    all_of(send2, two_sem.at[0])

    def sent(t, _):
        part = send3.at[t, pl.ds(0, n - 1)]
        pltpu.make_async_copy(part, part, del_s_sem).wait()
        return 0

    lax.fori_loop(0, tiles, sent, 0)


def shards(heads_in, writer, reader, log_decay, norm_gain, merge_weight, frame_owner):
    tokens, width = heads_in.shape
    n = lax.axis_size("span")
    chunks = tokens // CHUNK
    tiles = width // LANES
    frames = frame_owner.shape[0]
    state_size = writer.shape[1]
    deep, out_width = merge_weight.shape
    assert (n, state_size, width, out_width, frames) == (32, 64, 1536, 1536, 16)
    vmem, dma = pltpu.VMEM, pltpu.SemaphoreType.DMA
    in_place = pl.BlockSpec(memory_space=pltpu.HBM)
    return pl.pallas_call(
        functools.partial(kernel, n),
        out_shape=pltpu.VMEM((n * 16, out_width), BF16),
        in_specs=[in_place] * 7,
        out_specs=pl.BlockSpec(memory_space=pltpu.VMEM),
        scratch_shapes=[
            vmem((tiles, tokens, LANES), BF16),
            vmem(writer.shape[::-1], BF16),
            vmem(reader.shape[::-1], BF16),
            vmem(log_decay.shape[::-1], F32),
            vmem((width // 128, 128), F32),
            vmem((1, frames), jnp.int32),
            vmem((tiles, deep, LANES), BF16),
            vmem((2 * CHUNK, 3 * CHUNK), BF16),
            vmem((128, width), BF16),
            vmem((LANES, LANES), BF16),
            vmem((chunks, tiles, CHUNK + state_size, LANES), BF16),
            vmem((chunks, CHUNK + 16, 128), F32),
            vmem((chunks, 2 * CHUNK, 128), F32),
            vmem((chunks, 2 * CHUNK, 128), BF16),
            vmem((chunks, CHUNK, CHUNK + state_size), BF16),
            vmem((state_size, width), F32),
            vmem((tokens, state_size), BF16),
            vmem((tiles, tokens, LANES), F32),
            vmem((tiles, tokens, LANES), F32),
            vmem((tokens // 4, deep), BF16),
            vmem((1, 128), F32),
            vmem((n, 1, 128), F32),
            vmem((n, 8, 384), BF16),
            vmem((n, 8, 384), BF16),
            vmem((4, n, 384), F32),
            vmem((n, 8, 384), BF16),
            vmem((n, 8, 384), BF16),
            vmem((state_size, width), F32),
            vmem((n * 16, frames * 16), BF16),
            vmem((n * 16, n * 16), BF16),
            vmem((tiles, n, 16, LANES), BF16),
            vmem((tiles, n, 16, LANES), BF16),
            dma((tiles,)),
            dma((5,)),
            dma((tiles,)),
            dma((2,)),
            dma((2,)),
            dma((2,)),
            dma,
            dma((tiles,)),
        ],
        compiler_params=pltpu.CompilerParams(
            collective_id=0, has_side_effects=True, vmem_limit_bytes=54 * 1024 * 1024
        ),
    )(
        *(
            pltpu.with_memory_space_constraint(array, pltpu.HBM)
            for array in (
                heads_in,
                writer.T,
                reader.T,
                log_decay.T,
                norm_gain.reshape(width // 128, 128),
                frame_owner.reshape(1, frames),
                merge_weight,
            )
        )
    )


def solution(mesh):
    return jax.shard_map(
        shards,
        mesh=mesh,
        in_specs=(
            P(("batch", "span"), None),
            P(("batch", "span"), None),
            P(("batch", "span"), None),
            P(("batch", "span"), None),
            P(),
            P(),
            P(("batch", "span")),
        ),
        out_specs=P(("batch", "span"), None),
        check_vma=False,
    )
```

```python
import functools

import jax
import jax.numpy as jnp
from jax import lax
from jax.experimental import pallas as pl
from jax.experimental.pallas import tpu as pltpu
from jax.sharding import PartitionSpec as P

MESH = pl.DeviceIdType.MESH
F32 = jnp.float32
BF16 = jnp.bfloat16
EPSILON = 1e-05
FRAME_SIDE = 8
CHUNK = 128
LANES = 256
GROUP = 64


def dot(a, b):
    return lax.dot_general(a, b, (((1,), (0,)), ((), ())), preferred_element_type=F32)


def dot_t(a, b):
    return lax.dot_general(a, b, (((1,), (1,)), ((), ())), preferred_element_type=F32)


def iota(shape, axis):
    return lax.broadcasted_iota(jnp.int32, shape, axis)


def ones_where(condition):
    return jnp.where(condition, 1.0, 0.0).astype(BF16)


def slice_of(p):
    b = (p & 1) * 2 + ((p >> 1) & 1)
    return slice(8 * (p >> 2), 8 * (p >> 2) + 8), slice(384 * b, 384 * b + 384)


def token_of_row(row):
    q, rest = row >> 5, row & 31
    frame, i2, j2 = rest >> 4, (rest >> 2) & 3, rest & 3
    return frame * 64 + (2 * i2 + (q >> 1)) * 8 + 2 * j2 + (q & 1)


def widen(factor, tile):
    lane = tile * 8 + (iota(factor.shape, 1) >> 5)
    pick = functools.partial(jnp.take_along_axis, factor, axis=1, mode="promise_in_bounds")
    return jnp.concatenate([pick(lane), pick(lane + 4)], axis=1)


def two_parts(values):
    high = values.astype(BF16)
    low = (values - high.astype(F32)).astype(BF16)
    return jnp.where(iota(values.shape, 1) < 64, high.astype(F32), low.astype(F32)).astype(BF16)


def kernel(
    n, x_h, w_h, r_h, d_h, g_h, o_h, wm_h, out_h,
    x_v, w_v, r_v, d_v, g_v, o_v, wm_v,
    cum_l, expand, block_diag, xs_v, in_factor, out_arg, out_factor, left_v, state, rp_v, ml_v, od_v, a_v,
    meta_s, meta_r, send1, recv1, decays, send2, recv2, enter, sel_s, sel_r, send3, recv3,
    x_sem, in_sem, wm_sem, meta_sem, one_sem, two_sem, del_s_sem, del_r_sem,
):
    me = lax.axis_index("span")
    tokens, width = x_h.shape
    chunks = tokens // CHUNK
    heads = d_h.shape[0]
    tiles = width // LANES
    frames = o_h.shape[1]
    rows = 16

    small = [
        pltpu.make_async_copy(s, d, in_sem.at[k])
        for k, (s, d) in enumerate(((d_h, d_v), (w_h, w_v), (r_h, r_v), (g_h, g_v), (o_h, o_v)))
    ]

    def columns(t):
        return pl.ds(pl.multiple_of(t * LANES, LANES), LANES)

    def load(t):
        return pltpu.make_async_copy(x_h.at[:, columns(t)], x_v.at[t], x_sem.at[t])

    def load_weight(t):
        return pltpu.make_async_copy(wm_h.at[:, columns(t)], wm_v.at[t], wm_sem.at[t])

    for copy in small + [load(t) for t in range(tiles)]:
        copy.start()

    barrier = pltpu.get_barrier_semaphore()

    def greet(k, _):
        pl.semaphore_signal(
            barrier, inc=1, device_id={"span": lax.rem(me + k, n)}, device_id_type=MESH
        )
        return 0

    lax.fori_loop(1, n, greet, 0)

    row_l, col_l = iota((CHUNK, CHUNK), 0), iota((CHUNK, CHUNK), 1)
    token = token_of_row(row_l)
    lower = ones_where(col_l <= row_l)
    lower_p = ones_where(col_l <= token)
    for k in range(3):
        cum_l[0:CHUNK, k * CHUNK : (k + 1) * CHUNK] = lower
        cum_l[CHUNK : 2 * CHUNK, k * CHUNK : (k + 1) * CHUNK] = lower_p
    head_dim_shift = (width // heads).bit_length() - 1
    expand[...] = ones_where(
        (iota((128, width), 0) & 63) == (iota((128, width), 1) >> head_dim_shift)
    )
    for copy in small:
        copy.wait()

    before = jnp.zeros((1, 128), F32)
    for c in range(chunks):
        part = slice(c * CHUNK, (c + 1) * CHUNK)
        decay = d_v[:, part]
        high = decay.astype(BF16)
        left = decay - high.astype(F32)
        middle = left.astype(BF16)
        low = (left - middle.astype(F32)).astype(BF16)
        parts = jnp.concatenate([high, middle, low], axis=1)
        gap = jnp.zeros((64 - heads, parts.shape[1]), BF16)
        both = dot_t(cum_l[...], jnp.concatenate([parts, gap, parts, gap], axis=0))
        running, running_p = both[0:CHUNK], both[CHUNK : 2 * CHUNK]
        ref = running[CHUNK // 2 - 1 : CHUNK // 2]
        total = running[CHUNK - 1 : CHUNK]
        out_arg[c, 0:CHUNK] = running_p - ref
        out_arg[c, CHUNK : 2 * CHUNK] = running_p + before
        row = iota((16, 128), 0)
        extra = jnp.where(row == 0, ref, jnp.where(row == 1, total, total - ref))
        in_factor[c] = jnp.exp(jnp.concatenate([ref - running, extra], axis=0))
        before = before + total
    owners = o_v[...].astype(F32)
    own_row = jnp.concatenate(
        [jnp.zeros((1, 64), F32), owners, jnp.full((1, 64 - frames), -1.0, F32)], axis=1
    )
    meta_s[...] = jnp.where(iota((1, 128), 1) < 64, before, own_row)

    def summarize(t, _):
        load(t).wait()
        carry = jnp.zeros((w_v.shape[0], LANES), F32)
        full, scaled = {}, {}
        for k in range(chunks + 2):
            if k < chunks:
                full[k] = widen(in_factor[k], t)
            c = k - 1
            if 0 <= c < chunks:
                part = slice(c * CHUNK, (c + 1) * CHUNK)
                scaled[c] = (x_v[t, part].astype(F32) * full[c][0:CHUNK]).astype(BF16)
                xs_v[c, t, 0:CHUNK] = scaled[c]
            c = k - 2
            if c >= 0:
                own = dot(w_v[:, c * CHUNK : (c + 1) * CHUNK], scaled.pop(c))
                scales = full.pop(c)[CHUNK : CHUNK + 3]
                xs_v[c, t, CHUNK : CHUNK + 64] = (carry * scales[0:1]).astype(BF16)
                carry = carry * scales[1:2] + own * scales[2:3]
        state[:, columns(t)] = carry
        return 0

    def remote(source, target, sems, d):
        return pltpu.make_async_remote_copy(
            src_ref=source,
            dst_ref=target,
            send_sem=sems.at[0],
            recv_sem=sems.at[1],
            device_id={"span": d},
            device_id_type=MESH,
        )

    def all_of(ref, sem):
        part = ref.at[pl.ds(0, n - 1)]
        pltpu.make_async_copy(part, part, sem).wait()

    z, y, core = me // 8, lax.rem(me // 2, 4), lax.rem(me, 2)
    order = sorted(
        ((dz, dy, dc) for dz in range(4) for dy in range(4) for dc in range(2) if dz + dy + dc),
        key=lambda o: -min(o[0], 4 - o[0]) - min(o[1], 4 - o[1]),
    )

    def place_of(dz, dy, dc):
        return lax.rem(z + dz, 4) * 8 + lax.rem(y + dy, 4) * 2 + lax.rem(core + dc, 2)

    def send_meta(k, _):
        remote(meta_s, meta_r.at[me], meta_sem, lax.rem(me + k, n)).start()
        return 0

    def send_half(half):
        for p in range(half, n, 2):
            rows8, cols384 = slice_of(p)
            send1[p] = state[rows8, cols384].astype(BF16)

        for dz, dy, dc in order + [(0, 0, 0)]:
            if dc == 0:
                d = lax.rem(z + dz, 4) * 8 + lax.rem(y + dy, 4) * 2 + half

                @pl.when(d != me)
                def _():
                    remote(send1.at[d], recv1.at[me], one_sem, d).start()

    lax.fori_loop(0, tiles // 2, summarize, 0, unroll=3)
    pl.semaphore_wait(barrier, n - 1)
    lax.fori_loop(1, n, send_meta, 0)
    send_half(0)
    lax.fori_loop(tiles // 2, tiles, summarize, 0, unroll=3)
    send_half(1)
    for t in range(tiles):
        load_weight(t).start()
    meta_r[me] = meta_s[...]
    recv1[me] = send1[me]

    token = token_of_row(iota((CHUNK, CHUNK), 0))
    causal = iota((CHUNK, CHUNK), 1) <= token
    permute = ones_where(iota((CHUNK, CHUNK), 1) == token)

    for c in range(chunks):
        part = slice(c * CHUNK, (c + 1) * CHUNK)
        reads = dot_t(permute, r_v[:, part]).astype(BF16)
        scores = dot(reads, w_v[:, part])
        rp_v[part] = reads
        left_v[c] = jnp.concatenate([jnp.where(causal, scores, 0.0).astype(BF16), reads], axis=1)
        out_factor[c] = two_parts(jnp.exp(out_arg[c]))

    def local(t, _):
        spread = expand[:, columns(t)]
        for c in range(chunks):
            part = slice(c * CHUNK, (c + 1) * CHUNK)
            full = dot(out_factor[c], spread)
            ml_v[t, part] = dot(left_v[c], xs_v[c, t]) * full[0:CHUNK]
            od_v[t, part] = full[CHUNK : 2 * CHUNK]
        return 0

    lax.fori_loop(0, tiles // 2, local, 0)

    all_of(meta_r, meta_sem.at[1])
    meta = meta_r[:, 0, :]
    totals = meta[:, 0:64]
    factors = two_parts(jnp.exp(jnp.concatenate([totals, totals], axis=1)))
    for b in range(4):
        decays[b] = dot(factors, expand[:, 384 * b : 384 * b + 384])
    all_of(recv1, one_sem.at[1])
    quarter = lax.rem(me, 2) * 2 + lax.rem(me // 2, 2)
    carry = jnp.zeros(recv1.shape[1:], F32)
    for i in range(n):
        send2[i] = carry.astype(BF16)
        if i < n - 1:
            carry = carry * decays[quarter, i : i + 1, :] + recv1[i].astype(F32)

    for dz, dy, dc in order:
        d = place_of(dz, dy, dc)
        remote(send2.at[d], recv2.at[me], two_sem, d).start()
    recv2[me] = send2[me]
    lax.fori_loop(tiles // 2, tiles, local, 0)
    block_diag[...] = jnp.where(
        (iota((LANES, LANES), 0) >> 6) == (iota((LANES, LANES), 1) >> 6), 1.0 / GROUP, 0.0
    ).astype(BF16)
    owner_rows = jnp.broadcast_to(owners, (8, frames)).astype(BF16)
    spread = ones_where(
        iota((frames, frames * rows), 0) == (iota((frames, frames * rows), 1) >> 4)
    )
    owner_row = dot(owner_rows, spread)[0:1]
    shape = (n * rows, frames * rows)
    sel_s[...] = ones_where(
        ((iota(shape, 0) >> 4).astype(F32) == owner_row)
        & ((iota(shape, 0) & 15) == (iota(shape, 1) & 15))
    )
    mine = (meta == me.astype(F32)) & (iota(meta.shape, 1) >= 64)
    owned = jnp.max(jnp.where(mine, 1.0, 0.0), axis=1, keepdims=True)
    owned = jnp.broadcast_to(owned, (n, 128))
    rank = dot(ones_where(iota((n, n), 1) < iota((n, n), 0)), owned.astype(BF16))
    place = jnp.where(owned > 0.0, rank + 1.0, 0.0)[:, 0:1]
    shape = (n, n * rows)
    place_row = jnp.sum(
        jnp.where((iota(shape, 1) >> 4) == iota(shape, 0), place, 0.0), axis=0, keepdims=True
    )
    shape = (n * rows, n * rows)
    sel_r[...] = ones_where(
        (((iota(shape, 0) >> 4) + 1).astype(F32) == place_row)
        & ((iota(shape, 0) & 15) == (iota(shape, 1) & 15))
    )

    all_of(recv2, two_sem.at[1])
    for p in range(n):
        rows8, cols384 = slice_of(p)
        enter[rows8, cols384] = recv2[p].astype(F32)

    def norm(t, _):
        entering = enter[:, columns(t)].astype(BF16)
        gain = jnp.concatenate([g_v[pl.ds(2 * t, 1), :], g_v[pl.ds(2 * t + 1, 1), :]], axis=1)
        mixed, squares = {}, {}
        for k in range(chunks + 2):
            if k < chunks:
                part = slice(k * CHUNK, (k + 1) * CHUNK)
                mixed[k] = ml_v[t, part] + od_v[t, part] * dot(rp_v[part], entering)
            c = k - 1
            if 0 <= c < chunks:
                squares[c] = dot((mixed[c] * mixed[c]).astype(BF16), block_diag[...])
            c = k - 2
            if c >= 0:
                normed = mixed.pop(c) * lax.rsqrt(squares.pop(c) + EPSILON) * gain
                normed = normed.astype(BF16)
                for q in range(4):
                    first = pl.multiple_of(q * width + t * LANES, LANES)
                    a_v[c * 32 : (c + 1) * 32, pl.ds(first, LANES)] = normed[q * 32 : (q + 1) * 32]
        return 0

    lax.fori_loop(0, tiles, norm, 0, unroll=3)

    def deliver(t, _):
        load_weight(t).wait()
        merged = dot(a_v[...], wm_v[t]).astype(BF16)
        send3[t] = dot(sel_s[...], merged).astype(BF16).reshape(n, rows, LANES)

        for dz, dy, dc in order:
            d = place_of(dz, dy, dc)
            pltpu.make_async_remote_copy(
                src_ref=send3.at[t, d],
                dst_ref=recv3.at[t, me],
                send_sem=del_s_sem,
                recv_sem=del_r_sem.at[t],
                device_id={"span": d},
                device_id_type=MESH,
            ).start()
        recv3[t, me] = send3[t, me]
        return 0

    lax.fori_loop(0, tiles, deliver, 0)

    def arrive(t, _):
        part = recv3.at[t, pl.ds(0, n - 1)]
        pltpu.make_async_copy(part, part, del_r_sem.at[t]).wait()
        out_h[:, columns(t)] = dot(
            sel_r[...], recv3[t].reshape(n * rows, LANES)
        ).astype(BF16)
        return 0

    lax.fori_loop(0, tiles, arrive, 0)
    one_meta = meta_r.at[pl.ds(0, n - 1)]
    pltpu.make_async_copy(one_meta, one_meta, meta_sem.at[0]).wait()
    all_of(send1, one_sem.at[0])
    all_of(send2, two_sem.at[0])

    def sent(t, _):
        part = send3.at[t, pl.ds(0, n - 1)]
        pltpu.make_async_copy(part, part, del_s_sem).wait()
        return 0

    lax.fori_loop(0, tiles, sent, 0)


def shards(heads_in, writer, reader, log_decay, norm_gain, merge_weight, frame_owner):
    tokens, width = heads_in.shape
    n = lax.axis_size("span")
    chunks = tokens // CHUNK
    tiles = width // LANES
    frames = frame_owner.shape[0]
    state_size = writer.shape[1]
    deep, out_width = merge_weight.shape
    assert (n, state_size, width, out_width, frames) == (32, 64, 1536, 1536, 16)
    vmem, dma = pltpu.VMEM, pltpu.SemaphoreType.DMA
    in_place = pl.BlockSpec(memory_space=pltpu.HBM)
    return pl.pallas_call(
        functools.partial(kernel, n),
        out_shape=pltpu.VMEM((n * 16, out_width), BF16),
        in_specs=[in_place] * 7,
        out_specs=pl.BlockSpec(memory_space=pltpu.VMEM),
        scratch_shapes=[
            vmem((tiles, tokens, LANES), BF16),
            vmem(writer.shape[::-1], BF16),
            vmem(reader.shape[::-1], BF16),
            vmem(log_decay.shape[::-1], F32),
            vmem((width // 128, 128), F32),
            vmem((1, frames), jnp.int32),
            vmem((tiles, deep, LANES), BF16),
            vmem((2 * CHUNK, 3 * CHUNK), BF16),
            vmem((128, width), BF16),
            vmem((LANES, LANES), BF16),
            vmem((chunks, tiles, CHUNK + state_size, LANES), BF16),
            vmem((chunks, CHUNK + 16, 128), F32),
            vmem((chunks, 2 * CHUNK, 128), F32),
            vmem((chunks, 2 * CHUNK, 128), BF16),
            vmem((chunks, CHUNK, CHUNK + state_size), BF16),
            vmem((state_size, width), F32),
            vmem((tokens, state_size), BF16),
            vmem((tiles, tokens, LANES), F32),
            vmem((tiles, tokens, LANES), F32),
            vmem((tokens // 4, deep), BF16),
            vmem((1, 128), F32),
            vmem((n, 1, 128), F32),
            vmem((n, 8, 384), BF16),
            vmem((n, 8, 384), BF16),
            vmem((4, n, 384), F32),
            vmem((n, 8, 384), BF16),
            vmem((n, 8, 384), BF16),
            vmem((state_size, width), F32),
            vmem((n * 16, frames * 16), BF16),
            vmem((n * 16, n * 16), BF16),
            vmem((tiles, n, 16, LANES), BF16),
            vmem((tiles, n, 16, LANES), BF16),
            dma((tiles,)),
            dma((5,)),
            dma((tiles,)),
            dma((2,)),
            dma((2,)),
            dma((2,)),
            dma,
            dma((tiles,)),
        ],
        compiler_params=pltpu.CompilerParams(
            collective_id=0, has_side_effects=True, vmem_limit_bytes=54 * 1024 * 1024
        ),
    )(
        *(
            pltpu.with_memory_space_constraint(array, pltpu.HBM)
            for array in (
                heads_in,
                writer.T,
                reader.T,
                log_decay.T,
                norm_gain.reshape(width // 128, 128),
                frame_owner.reshape(1, frames),
                merge_weight,
            )
        )
    )


def solution(mesh):
    return jax.shard_map(
        shards,
        mesh=mesh,
        in_specs=(
            P(("batch", "span"), None),
            P(("batch", "span"), None),
            P(("batch", "span"), None),
            P(("batch", "span"), None),
            P(),
            P(),
            P(("batch", "span")),
        ),
        out_specs=P(("batch", "span"), None),
        check_vma=False,
    )
```

```python
import functools

import jax
import jax.numpy as jnp
from jax import lax
from jax.experimental import pallas as pl
from jax.experimental.pallas import tpu as pltpu
from jax.sharding import PartitionSpec as P

MESH = pl.DeviceIdType.MESH
F32 = jnp.float32
BF16 = jnp.bfloat16
EPSILON = 1e-05
FRAME_SIDE = 8
CHUNK = 128
LANES = 256
GROUP = 64


def dot(a, b):
    return lax.dot_general(a, b, (((1,), (0,)), ((), ())), preferred_element_type=F32)


def dot_t(a, b):
    return lax.dot_general(a, b, (((1,), (1,)), ((), ())), preferred_element_type=F32)


def iota(shape, axis):
    return lax.broadcasted_iota(jnp.int32, shape, axis)


def ones_where(condition):
    return jnp.where(condition, 1.0, 0.0).astype(BF16)


def slice_of(p):
    b = (p & 1) * 2 + ((p >> 1) & 1)
    return slice(8 * (p >> 2), 8 * (p >> 2) + 8), slice(384 * b, 384 * b + 384)


def token_of_row(row):
    q, rest = row >> 5, row & 31
    frame, i2, j2 = rest >> 4, (rest >> 2) & 3, rest & 3
    return frame * 64 + (2 * i2 + (q >> 1)) * 8 + 2 * j2 + (q & 1)


def widen(factor, tile):
    lane = tile * 8 + (iota(factor.shape, 1) >> 5)
    pick = functools.partial(jnp.take_along_axis, factor, axis=1, mode="promise_in_bounds")
    return jnp.concatenate([pick(lane), pick(lane + 4)], axis=1)


def two_parts(values):
    high = values.astype(BF16)
    low = (values - high.astype(F32)).astype(BF16)
    return jnp.where(iota(values.shape, 1) < 64, high.astype(F32), low.astype(F32)).astype(BF16)


def kernel(
    n, x_h, w_h, r_h, d_h, g_h, o_h, wm_h, out_h,
    x_v, w_v, r_v, d_v, g_v, o_v, wm_v,
    cum_l, expand, block_diag, xs_v, in_factor, out_arg, out_factor, left_v, state, rp_v, ml_v, od_v, a_v,
    meta_s, meta_r, send1, recv1, decays, send2, recv2, enter, sel_s, sel_r, send3, recv3,
    x_sem, in_sem, wm_sem, meta_sem, one_sem, two_sem, del_s_sem, del_r_sem,
):
    me = lax.axis_index("span")
    tokens, width = x_h.shape
    chunks = tokens // CHUNK
    heads = d_h.shape[0]
    tiles = width // LANES
    frames = o_h.shape[1]
    rows = 16

    small = [
        pltpu.make_async_copy(s, d, in_sem.at[k])
        for k, (s, d) in enumerate(((d_h, d_v), (w_h, w_v), (r_h, r_v), (g_h, g_v), (o_h, o_v)))
    ]

    def columns(t):
        return pl.ds(pl.multiple_of(t * LANES, LANES), LANES)

    def load(t):
        return pltpu.make_async_copy(x_h.at[:, columns(t)], x_v.at[t], x_sem.at[t])

    def load_weight(t):
        return pltpu.make_async_copy(wm_h.at[:, columns(t)], wm_v.at[t], wm_sem.at[t])

    for copy in small + [load(t) for t in range(tiles)]:
        copy.start()

    barrier = pltpu.get_barrier_semaphore()

    def greet(k, _):
        pl.semaphore_signal(
            barrier, inc=1, device_id={"span": lax.rem(me + k, n)}, device_id_type=MESH
        )
        return 0

    lax.fori_loop(1, n, greet, 0)

    row_l, col_l = iota((CHUNK, CHUNK), 0), iota((CHUNK, CHUNK), 1)
    token = token_of_row(row_l)
    lower = ones_where(col_l <= row_l)
    lower_p = ones_where(col_l <= token)
    for k in range(3):
        cum_l[0:CHUNK, k * CHUNK : (k + 1) * CHUNK] = lower
        cum_l[CHUNK : 2 * CHUNK, k * CHUNK : (k + 1) * CHUNK] = lower_p
    head_dim_shift = (width // heads).bit_length() - 1
    expand[...] = ones_where(
        (iota((128, width), 0) & 63) == (iota((128, width), 1) >> head_dim_shift)
    )
    for copy in small:
        copy.wait()

    before = jnp.zeros((1, 128), F32)
    for c in range(chunks):
        part = slice(c * CHUNK, (c + 1) * CHUNK)
        decay = d_v[:, part]
        high = decay.astype(BF16)
        left = decay - high.astype(F32)
        middle = left.astype(BF16)
        low = (left - middle.astype(F32)).astype(BF16)
        parts = jnp.concatenate([high, middle, low], axis=1)
        gap = jnp.zeros((64 - heads, parts.shape[1]), BF16)
        both = dot_t(cum_l[...], jnp.concatenate([parts, gap, parts, gap], axis=0))
        running, running_p = both[0:CHUNK], both[CHUNK : 2 * CHUNK]
        ref = running[CHUNK // 2 - 1 : CHUNK // 2]
        total = running[CHUNK - 1 : CHUNK]
        out_arg[c, 0:CHUNK] = running_p - ref
        out_arg[c, CHUNK : 2 * CHUNK] = running_p + before
        row = iota((16, 128), 0)
        extra = jnp.where(row == 0, ref, jnp.where(row == 1, total, total - ref))
        in_factor[c] = jnp.exp(jnp.concatenate([ref - running, extra], axis=0))
        before = before + total
    owners = o_v[...].astype(F32)
    own_row = jnp.concatenate(
        [jnp.zeros((1, 64), F32), owners, jnp.full((1, 64 - frames), -1.0, F32)], axis=1
    )
    meta_s[...] = jnp.where(iota((1, 128), 1) < 64, before, own_row)

    def summarize(t, _):
        load(t).wait()
        carry = jnp.zeros((w_v.shape[0], LANES), F32)
        full, scaled = {}, {}
        for k in range(chunks + 2):
            if k < chunks:
                full[k] = widen(in_factor[k], t)
            c = k - 1
            if 0 <= c < chunks:
                part = slice(c * CHUNK, (c + 1) * CHUNK)
                scaled[c] = (x_v[t, part].astype(F32) * full[c][0:CHUNK]).astype(BF16)
                xs_v[c, t, 0:CHUNK] = scaled[c]
            c = k - 2
            if c >= 0:
                own = dot(w_v[:, c * CHUNK : (c + 1) * CHUNK], scaled.pop(c))
                scales = full.pop(c)[CHUNK : CHUNK + 3]
                xs_v[c, t, CHUNK : CHUNK + 64] = (carry * scales[0:1]).astype(BF16)
                carry = carry * scales[1:2] + own * scales[2:3]
        state[:, columns(t)] = carry
        return 0

    def remote(source, target, sems, d):
        return pltpu.make_async_remote_copy(
            src_ref=source,
            dst_ref=target,
            send_sem=sems.at[0],
            recv_sem=sems.at[1],
            device_id={"span": d},
            device_id_type=MESH,
        )

    def all_of(ref, sem):
        part = ref.at[pl.ds(0, n - 1)]
        pltpu.make_async_copy(part, part, sem).wait()

    z, y, core = me // 8, lax.rem(me // 2, 4), lax.rem(me, 2)
    order = sorted(
        ((dz, dy, dc) for dz in range(4) for dy in range(4) for dc in range(2) if dz + dy + dc),
        key=lambda o: -min(o[0], 4 - o[0]) - min(o[1], 4 - o[1]),
    )

    def place_of(dz, dy, dc):
        return lax.rem(z + dz, 4) * 8 + lax.rem(y + dy, 4) * 2 + lax.rem(core + dc, 2)

    def send_meta(k, _):
        remote(meta_s, meta_r.at[me], meta_sem, lax.rem(me + k, n)).start()
        return 0

    def send_half(half):
        for p in range(half, n, 2):
            rows8, cols384 = slice_of(p)
            send1[p] = state[rows8, cols384].astype(BF16)

        for dz, dy, dc in order + [(0, 0, 0)]:
            if dc == 0:
                d = lax.rem(z + dz, 4) * 8 + lax.rem(y + dy, 4) * 2 + half

                @pl.when(d != me)
                def _():
                    remote(send1.at[d], recv1.at[me], one_sem, d).start()

    lax.fori_loop(0, tiles // 2, summarize, 0, unroll=3)
    pl.semaphore_wait(barrier, n - 1)
    lax.fori_loop(1, n, send_meta, 0)
    send_half(0)
    lax.fori_loop(tiles // 2, tiles, summarize, 0, unroll=3)
    send_half(1)
    for t in range(tiles):
        load_weight(t).start()
    meta_r[me] = meta_s[...]
    recv1[me] = send1[me]

    token = token_of_row(iota((CHUNK, CHUNK), 0))
    causal = iota((CHUNK, CHUNK), 1) <= token
    permute = ones_where(iota((CHUNK, CHUNK), 1) == token)

    for c in range(chunks):
        part = slice(c * CHUNK, (c + 1) * CHUNK)
        reads = dot_t(permute, r_v[:, part]).astype(BF16)
        scores = dot(reads, w_v[:, part])
        rp_v[part] = reads
        left_v[c] = jnp.concatenate([jnp.where(causal, scores, 0.0).astype(BF16), reads], axis=1)
        out_factor[c] = two_parts(jnp.exp(out_arg[c]))

    def local(t, _):
        spread = expand[:, columns(t)]
        for c in range(chunks):
            part = slice(c * CHUNK, (c + 1) * CHUNK)
            full = dot(out_factor[c], spread)
            ml_v[t, part] = dot(left_v[c], xs_v[c, t]) * full[0:CHUNK]
            od_v[t, part] = full[CHUNK : 2 * CHUNK]
        return 0

    lax.fori_loop(0, tiles // 2, local, 0)

    all_of(meta_r, meta_sem.at[1])
    meta = meta_r[:, 0, :]
    totals = meta[:, 0:64]
    factors = two_parts(jnp.exp(jnp.concatenate([totals, totals], axis=1)))
    for b in range(4):
        decays[b] = dot(factors, expand[:, 384 * b : 384 * b + 384])
    all_of(recv1, one_sem.at[1])
    quarter = lax.rem(me, 2) * 2 + lax.rem(me // 2, 2)
    carry = jnp.zeros(recv1.shape[1:], F32)
    for i in range(n):
        send2[i] = carry.astype(BF16)
        if i < n - 1:
            carry = carry * decays[quarter, i : i + 1, :] + recv1[i].astype(F32)

    for dz, dy, dc in order:
        d = place_of(dz, dy, dc)
        remote(send2.at[d], recv2.at[me], two_sem, d).start()
    recv2[me] = send2[me]
    lax.fori_loop(tiles // 2, tiles, local, 0)
    block_diag[...] = jnp.where(
        (iota((LANES, LANES), 0) >> 6) == (iota((LANES, LANES), 1) >> 6), 1.0 / GROUP, 0.0
    ).astype(BF16)
    owner_rows = jnp.broadcast_to(owners, (8, frames)).astype(BF16)
    spread = ones_where(
        iota((frames, frames * rows), 0) == (iota((frames, frames * rows), 1) >> 4)
    )
    owner_row = dot(owner_rows, spread)[0:1]
    shape = (n * rows, frames * rows)
    sel_s[...] = ones_where(
        ((iota(shape, 0) >> 4).astype(F32) == owner_row)
        & ((iota(shape, 0) & 15) == (iota(shape, 1) & 15))
    )
    mine = (meta == me.astype(F32)) & (iota(meta.shape, 1) >= 64)
    owned = jnp.max(jnp.where(mine, 1.0, 0.0), axis=1, keepdims=True)
    owned = jnp.broadcast_to(owned, (n, 128))
    rank = dot(ones_where(iota((n, n), 1) < iota((n, n), 0)), owned.astype(BF16))
    place = jnp.where(owned > 0.0, rank + 1.0, 0.0)[:, 0:1]
    shape = (n, n * rows)
    place_row = jnp.sum(
        jnp.where((iota(shape, 1) >> 4) == iota(shape, 0), place, 0.0), axis=0, keepdims=True
    )
    shape = (n * rows, n * rows)
    sel_r[...] = ones_where(
        (((iota(shape, 0) >> 4) + 1).astype(F32) == place_row)
        & ((iota(shape, 0) & 15) == (iota(shape, 1) & 15))
    )

    all_of(recv2, two_sem.at[1])
    for p in range(n):
        rows8, cols384 = slice_of(p)
        enter[rows8, cols384] = recv2[p].astype(F32)

    def norm(t, _):
        entering = enter[:, columns(t)].astype(BF16)
        gain = jnp.concatenate([g_v[pl.ds(2 * t, 1), :], g_v[pl.ds(2 * t + 1, 1), :]], axis=1)
        mixed, squares = {}, {}
        for k in range(chunks + 2):
            if k < chunks:
                part = slice(k * CHUNK, (k + 1) * CHUNK)
                mixed[k] = ml_v[t, part] + od_v[t, part] * dot(rp_v[part], entering)
            c = k - 1
            if 0 <= c < chunks:
                squares[c] = dot((mixed[c] * mixed[c]).astype(BF16), block_diag[...])
            c = k - 2
            if c >= 0:
                normed = mixed.pop(c) * lax.rsqrt(squares.pop(c) + EPSILON) * gain
                normed = normed.astype(BF16)
                for q in range(4):
                    first = pl.multiple_of(q * width + t * LANES, LANES)
                    a_v[c * 32 : (c + 1) * 32, pl.ds(first, LANES)] = normed[q * 32 : (q + 1) * 32]
        return 0

    lax.fori_loop(0, tiles, norm, 0, unroll=6)

    def deliver(t, _):
        load_weight(t).wait()
        merged = dot(a_v[...], wm_v[t]).astype(BF16)
        send3[t] = dot(sel_s[...], merged).astype(BF16).reshape(n, rows, LANES)

        for dz, dy, dc in order:
            d = place_of(dz, dy, dc)
            pltpu.make_async_remote_copy(
                src_ref=send3.at[t, d],
                dst_ref=recv3.at[t, me],
                send_sem=del_s_sem,
                recv_sem=del_r_sem.at[t],
                device_id={"span": d},
                device_id_type=MESH,
            ).start()
        recv3[t, me] = send3[t, me]
        return 0

    lax.fori_loop(0, tiles, deliver, 0)

    def arrive(t, _):
        part = recv3.at[t, pl.ds(0, n - 1)]
        pltpu.make_async_copy(part, part, del_r_sem.at[t]).wait()
        out_h[:, columns(t)] = dot(
            sel_r[...], recv3[t].reshape(n * rows, LANES)
        ).astype(BF16)
        return 0

    lax.fori_loop(0, tiles, arrive, 0)
    one_meta = meta_r.at[pl.ds(0, n - 1)]
    pltpu.make_async_copy(one_meta, one_meta, meta_sem.at[0]).wait()
    all_of(send1, one_sem.at[0])
    all_of(send2, two_sem.at[0])

    def sent(t, _):
        part = send3.at[t, pl.ds(0, n - 1)]
        pltpu.make_async_copy(part, part, del_s_sem).wait()
        return 0

    lax.fori_loop(0, tiles, sent, 0)


def shards(heads_in, writer, reader, log_decay, norm_gain, merge_weight, frame_owner):
    tokens, width = heads_in.shape
    n = lax.axis_size("span")
    chunks = tokens // CHUNK
    tiles = width // LANES
    frames = frame_owner.shape[0]
    state_size = writer.shape[1]
    deep, out_width = merge_weight.shape
    assert (n, state_size, width, out_width, frames) == (32, 64, 1536, 1536, 16)
    vmem, dma = pltpu.VMEM, pltpu.SemaphoreType.DMA
    in_place = pl.BlockSpec(memory_space=pltpu.HBM)
    return pl.pallas_call(
        functools.partial(kernel, n),
        out_shape=pltpu.VMEM((n * 16, out_width), BF16),
        in_specs=[in_place] * 7,
        out_specs=pl.BlockSpec(memory_space=pltpu.VMEM),
        scratch_shapes=[
            vmem((tiles, tokens, LANES), BF16),
            vmem(writer.shape[::-1], BF16),
            vmem(reader.shape[::-1], BF16),
            vmem(log_decay.shape[::-1], F32),
            vmem((width // 128, 128), F32),
            vmem((1, frames), jnp.int32),
            vmem((tiles, deep, LANES), BF16),
            vmem((2 * CHUNK, 3 * CHUNK), BF16),
            vmem((128, width), BF16),
            vmem((LANES, LANES), BF16),
            vmem((chunks, tiles, CHUNK + state_size, LANES), BF16),
            vmem((chunks, CHUNK + 16, 128), F32),
            vmem((chunks, 2 * CHUNK, 128), F32),
            vmem((chunks, 2 * CHUNK, 128), BF16),
            vmem((chunks, CHUNK, CHUNK + state_size), BF16),
            vmem((state_size, width), F32),
            vmem((tokens, state_size), BF16),
            vmem((tiles, tokens, LANES), F32),
            vmem((tiles, tokens, LANES), F32),
            vmem((tokens // 4, deep), BF16),
            vmem((1, 128), F32),
            vmem((n, 1, 128), F32),
            vmem((n, 8, 384), BF16),
            vmem((n, 8, 384), BF16),
            vmem((4, n, 384), F32),
            vmem((n, 8, 384), BF16),
            vmem((n, 8, 384), BF16),
            vmem((state_size, width), F32),
            vmem((n * 16, frames * 16), BF16),
            vmem((n * 16, n * 16), BF16),
            vmem((tiles, n, 16, LANES), BF16),
            vmem((tiles, n, 16, LANES), BF16),
            dma((tiles,)),
            dma((5,)),
            dma((tiles,)),
            dma((2,)),
            dma((2,)),
            dma((2,)),
            dma,
            dma((tiles,)),
        ],
        compiler_params=pltpu.CompilerParams(
            collective_id=0, has_side_effects=True, vmem_limit_bytes=54 * 1024 * 1024
        ),
    )(
        *(
            pltpu.with_memory_space_constraint(array, pltpu.HBM)
            for array in (
                heads_in,
                writer.T,
                reader.T,
                log_decay.T,
                norm_gain.reshape(width // 128, 128),
                frame_owner.reshape(1, frames),
                merge_weight,
            )
        )
    )


def solution(mesh):
    return jax.shard_map(
        shards,
        mesh=mesh,
        in_specs=(
            P(("batch", "span"), None),
            P(("batch", "span"), None),
            P(("batch", "span"), None),
            P(("batch", "span"), None),
            P(),
            P(),
            P(("batch", "span")),
        ),
        out_specs=P(("batch", "span"), None),
        check_vma=False,
    )
```
